128 devices in a mesh: gx: 8 (over x_hi, z), gy: 16 (over x_lo, y, core).
Axes of the slice: x: 4 (x_hi: 2, x_lo: 2; x = x_hi * 2 + x_lo), y: 4, z: 4, core: 2. Of those that a mesh axis runs over, the one named last changes fastest.
Arguments:
- velocity: float32 [3, 4, 1024, 1024], P(None, None, 'gy', 'gx'), may hold values from -6 to 6
- stress: float32 [3, 3, 4, 1024, 1024], P(None, None, None, 'gy', 'gx'), may hold values from -2.4 to 2.4
- face_mask: int32 [3, 4, 1024, 1024], P(None, None, 'gy', 'gx'), may hold values 0 or 1
- zones: int32 [4, 1024, 1024], P(None, 'gy', 'gx'), may hold values from 0 to 7
- zone_table: float32 [3, 8], replicated, may hold values from 0.5 to 2
- impedance: float32 [2, 3, 1024, 1024], P(None, None, ('gx', 'gy')), may hold values from 0.5 to 2
- memory: float32 [2, 31, 1024, 1024], P(None, None, ('gx', 'gy')), may hold values from -0.9 to 0.9
- history: float32 [2, 3, 31, 2, 1024, 1024], P(None, None, None, None, ('gx', 'gy')), may hold values from -6 to 6
Outputs:
- new_velocity: float32 [3, 4, 1024, 1024], P(None, None, 'gy', 'gx')
- new_stress: float32 [3, 3, 4, 1024, 1024], P(None, None, None, 'gy', 'gx')
The draws below stay inside these ranges and needn't reach their ends.
All inputs are finite; a program needn't handle non-finite values. No bound on the sum of `face_mask` on one device may be relied on, other than what follows from the above.
Results may differ from the reference program's by a relative error of at most 0.0001.
Values sent between devices are 32-bit elements; how exact they have to be, the bound alone decides.
No kernel may reach another device: no remote copies, remote signals or barrier semaphores. Data moves between devices by JAX's collectives and lax.ppermute only.
A program may use at most 128 MiB of HBM per device.

```python
import math
import jax
import jax.numpy as jnp
from jax import lax

NX = 1024
NY = 1024
LAYERS = 4
LAGS = 32
ZONES = 8
STEPS = 2


def set_ends(result, own_key, least, top_value):
    dims = result.shape
    index_at = [jax.random.randint(jax.random.fold_in(own_key, axis), (), 0, dims[axis]) for axis in range(len(dims))]
    result = result.at[tuple(index_at)].set(least)
    longest = dims.index(max(dims))
    index_at[longest] = (index_at[longest] + 1) % dims[longest]
    return result.at[tuple(index_at)].set(top_value)


def shard_levels(own_key, shape, split, low, top_value):
    def one(position, parts):
        heights = jax.random.uniform(jax.random.fold_in(jax.random.fold_in(own_key, 6), position), (parts,), jnp.float32, low / len(split), top_value / len(split))
        return jnp.repeat(jnp.exp(heights), shape[position] // parts).reshape((-1,) + (1,) * (len(shape) - position - 1))

    gain = one(*split[0])
    for cut in split[1:]:
        gain = gain * one(*cut)
    return gain


def scatter_about(rng, extent, width, reach, split=(), kind=jnp.bfloat16):
    gain = shard_levels(rng, extent, split, -0.22, 0.18) if split else 1.0
    array = jax.random.normal(rng, extent, jnp.float32) * width * gain
    return jnp.minimum(jnp.maximum(array, -reach), reach).astype(kind)


def setup_inputs(seed: int = 0) -> dict:
    key_list = jax.random.split(jax.random.key(seed), 9)
    return {
        "velocity": scatter_about(key_list[0], (3, LAYERS, NY, NX), 1.0, 6.0, ((2, 16), (3, 8)), jnp.float32),
        "stress": scatter_about(key_list[1], (3, 3, LAYERS, NY, NX), 0.4, 2.4, ((3, 16), (4, 8)), jnp.float32),
        "face_mask": set_ends((jax.random.randint(key_list[2], (3, LAYERS, NY, NX), 0, 8) < 7).astype(jnp.int32), jax.random.fold_in(key_list[2], 1), 0, 1),
        "zones": set_ends(jax.random.randint(key_list[3], (LAYERS, NY, NX), 0, ZONES), jax.random.fold_in(key_list[3], 1), 0, ZONES - 1).astype(jnp.int32),
        "zone_table": jnp.clip(jax.random.uniform(key_list[4], (3, ZONES), jnp.float32, 0.5, 2.0), 0.5, 2.0),
        "impedance": jnp.clip(jnp.exp(math.log(2.0) - 1.3862944 * jax.random.uniform(key_list[5], (2, 3, NX, NY), jnp.float32) ** shard_levels(key_list[5], (2, 3, NX, NY), ((2, 128),), -0.2, 0.2)), 0.5, 2.0),
        "memory": scatter_about(key_list[6], (2, LAGS - 1, NX, NY), 0.15, 0.9, ((2, 128),), jnp.float32),
        "history": scatter_about(key_list[7], (2, 3, LAGS - 1, 2, NX, NY), 1.0, 6.0, ((4, 128),), jnp.float32),
    }


time_step = 0.2

def respond(planes, impedance, memory, history, recent):
    spectrum = jnp.swapaxes(jnp.fft.fft2(planes, norm='ortho'), 2, 3)
    spectrum = jnp.stack([jnp.real(spectrum), jnp.imag(spectrum)], axis=2).astype(planes.dtype)
    step_index = len(recent)
    response = -impedance[:, :, None] * spectrum
    for offset in range(1, step_index + 1):
        response = response + memory[:, offset - 1][:, None, None] * recent[step_index - offset]
    for offset in range(step_index + 1, LAGS):
        response = response + memory[:, offset - 1][:, None, None] * history[:, :, offset - 1 - step_index]
    joined = lax.complex(response[:, :, 0], response[:, :, 1])
    traction = jnp.real(jnp.fft.ifft2(jnp.swapaxes(joined, 2, 3), norm='ortho')).astype(planes.dtype)
    return (traction, spectrum)

def reference(velocity, stress, face_mask, zones, zone_table, impedance, memory, history):
    rigidity = zone_table[0][zones]
    buoyancy = zone_table[1][zones]
    cohesion = zone_table[2][zones]
    cohesive = face_mask.astype(velocity.dtype)
    recent = []
    for step_index in range(STEPS):
        planes = jnp.stack([velocity[:, 0], velocity[:, -1]])
        traction, spectrum = respond(planes, impedance, memory, history, recent)
        recent.append(spectrum)
        along_x, along_y, along_z = (stress[:, 0], stress[:, 1], stress[:, 2])
        face_top = jnp.concatenate([along_z[:, :-1], traction[1][:, None]], axis=1)
        face_low = jnp.concatenate([traction[0][:, None], face_top[:, :-1]], axis=1)
        behind_x = jnp.roll(along_x, 1, axis=3)
        behind_y = jnp.roll(along_y, 1, axis=2)
        velocity = velocity + time_step * buoyancy * (along_x - behind_x + along_y - behind_y + face_top - face_low)
        ahead_x = jnp.roll(velocity, -1, axis=3)
        ahead_y = jnp.roll(velocity, -1, axis=2)
        new_x = cohesive[0] * (along_x + time_step * rigidity * (ahead_x - velocity))
        new_y = cohesive[1] * (along_y + time_step * rigidity * (ahead_y - velocity))
        inner_z = along_z[:, :-1] + time_step * rigidity[:-1] * (velocity[:, 1:] - velocity[:, :-1])
        new_z = cohesive[2] * jnp.concatenate([inner_z, traction[1][:, None]], axis=1)
        squares = lax.optimization_barrier(jnp.sum(new_x * new_x + new_y * new_y + new_z * new_z, axis=0))
        factor = cohesion / jnp.maximum(jnp.sqrt(squares), cohesion)
        stress = jnp.stack([new_x, new_y, new_z], axis=1) * factor
    return (velocity, stress)
```

```python
import functools
import math

import jax
import jax.numpy as jnp
import numpy as np
from jax import lax
from jax.experimental import pallas as pl
from jax.experimental.pallas import tpu as pltpu
from jax.sharding import PartitionSpec as P

time_step = 0.2
GX = 8
GY = 16
PEERS = 128
f32 = jnp.float32
bf16 = jnp.bfloat16
both = ("gx", "gy")
half_root = math.sqrt(0.5)


def halves(table):
    high = jnp.asarray(table, f32).astype(bf16)
    low = (jnp.asarray(table, f32) - high.astype(f32)).astype(bf16)
    return jnp.stack([high, low])


def tables():
    index = np.arange(PEERS)
    angle = 2.0 * np.pi * (np.outer(index, index) % PEERS) / PEERS
    c, s = np.cos(angle) / 32.0, np.sin(angle) / 32.0
    along_x = np.block([[c, s], [-s, c]])
    place = 8 * (index % GY) + index // GY
    angle = 2.0 * np.pi * (np.outer(place, index) % PEERS) / PEERS
    c, s = np.cos(angle) / 32.0, np.sin(angle) / 32.0
    along_y = np.block([[c, -s], [s, c]])
    turn = 2.0 * np.pi * np.outer(np.arange(8), index) / 1024.0
    twist = np.stack([np.cos(turn), np.sin(turn)])
    twist = np.broadcast_to(twist[:, :, None, :], (2, 8, 8, PEERS))
    return halves(along_x), halves(along_y), jnp.asarray(twist, f32)


def plus(a, b):
    imag = a[1] if b[1] is None else b[1] if a[1] is None else a[1] + b[1]
    return (a[0] + b[0], imag)


def minus(a, b):
    imag = a[1] if b[1] is None else -b[1] if a[1] is None else a[1] - b[1]
    return (a[0] - b[0], imag)


def turned(a, sign):
    if a[1] is None:
        return (jnp.zeros_like(a[0]), a[0] if sign > 0 else -a[0])
    return (-a[1], a[0]) if sign > 0 else (a[1], -a[0])


def four(x, sign):
    a, b = plus(x[0], x[2]), minus(x[0], x[2])
    c, d = plus(x[1], x[3]), turned(minus(x[1], x[3]), sign)
    return [plus(a, c), plus(b, d), minus(a, c), minus(b, d)]


def eight(x, sign):
    even, odd = four(x[0::2], sign), four(x[1::2], sign)
    o1, o3 = odd[1], odd[3]
    odd1 = ((o1[0] - sign * o1[1]) * half_root, (o1[1] + sign * o1[0]) * half_root)
    odd3 = ((-o3[0] - sign * o3[1]) * half_root, (sign * o3[0] - o3[1]) * half_root)
    odd = [odd[0], odd1, turned(odd[2], sign), odd3]
    return [plus(e, o) for e, o in zip(even, odd)] + [minus(e, o) for e, o in zip(even, odd)]


def split(x):
    high = x.astype(bf16)
    return high, (x - high.astype(f32)).astype(bf16)


def product(a, b, dims):
    dot = functools.partial(lax.dot_general, dimension_numbers=(dims, ((), ())), preferred_element_type=f32)
    return dot(a[0], b[0]) + (dot(a[1], b[0]) + dot(a[0], b[1]))


def from_peers(x_ref, pair, matrix, re_ref, im_ref, tiles):
    x = jnp.concatenate([x_ref[pl.ds(2 * pair + part, PEERS, stride=tiles), :] for part in range(2)], axis=0)
    y = product(split(x), matrix, ((0,), (0,)))
    re_ref[...] = y[:, :PEERS]
    im_ref[...] = y[:, PEERS:]


def to_peers(o_ref, pair, matrix, re_ref, im_ref, tiles):
    t = split(jnp.concatenate([re_ref[...], im_ref[...]], axis=1))
    out = product(matrix, t, ((1,), (1,)))
    for part in range(2):
        o_ref[pl.ds(2 * pair + part, PEERS, stride=tiles), :] = out[part * PEERS : (part + 1) * PEERS]


def twisted(value, twist_ref, index, sign):
    if index == 0:
        return value
    c, s = twist_ref[0, index], twist_ref[1, index]
    if sign < 0:
        return (value[0] * c + value[1] * s, value[1] * c - value[0] * s)
    return (value[0] * c - value[1] * s, value[1] * c + value[0] * s)


def strike_forward(take, twist_ref, matrix, o_ref, re_ref, im_ref):
    for pair in range(3):
        for member in range(2):
            plane = 2 * pair + member
            waves = eight([(take(plane, tile), None) for tile in range(GX)], -1.0)
            for k in range(8):
                re, im = waves[k]
                if im is None:
                    im = jnp.zeros_like(re)
                re, im = twisted((re, im), twist_ref, k, -1)
                rows = pl.ds(member * 64 + k * 8, 8)
                re_ref[rows, :] = re
                im_ref[rows, :] = im
        to_peers(o_ref, pair, matrix, re_ref, im_ref, 6)


def strike_inverse(x_ref, twist_ref, matrix, re_ref, im_ref, put):
    for pair in range(3):
        from_peers(x_ref, pair, matrix, re_ref, im_ref, 6)
        for member in range(2):
            values = []
            for k in range(8):
                rows = pl.ds(member * 64 + k, 8, stride=8)
                values.append(twisted((re_ref[rows, :], im_ref[rows, :]), twist_ref, k, 1))
            field = eight(values, 1.0)
            for tile in range(GX):
                put(2 * pair + member, tile, field[tile][0])


def forward_kernel(x_ref, mx_ref, twist_ref, o_ref, re_ref, im_ref):
    matrix = (mx_ref[0], mx_ref[1])
    take = lambda plane, tile: x_ref[tile, pl.ds(plane * 8, 8), :]
    strike_forward(take, twist_ref, matrix, o_ref, re_ref, im_ref)


def dip_kernel(carry, x_ref, impedance_ref, tail_ref, *refs):
    if carry:
        first_ref, later_ref, my_ref, twist_ref, o_ref, next_ref, re_ref, im_ref = refs
    else:
        my_ref, twist_ref, o_ref, re_ref, im_ref = refs
    matrix = (my_ref[0], my_ref[1])
    for pair in range(3):
        from_peers(x_ref, pair, matrix, re_ref, im_ref, 6)
        for member in range(2):
            plane = 2 * pair + member
            values = []
            for j in range(8):
                rows = pl.ds(member * 64 + j, 8, stride=8)
                values.append(twisted((re_ref[rows, :], im_ref[rows, :]), twist_ref, j, -1))
            spectrum = eight(values, -1.0)
            response = []
            for tile in range(8):
                lanes = pl.ds(tile * PEERS, PEERS)
                z = impedance_ref[plane, :, lanes]
                re, im = spectrum[tile]
                response.append(
                    (tail_ref[2 * plane, :, lanes] - z * re, tail_ref[2 * plane + 1, :, lanes] - z * im)
                )
                if carry:
                    first = first_ref[plane // 3, :, lanes]
                    next_ref[2 * plane, :, lanes] = later_ref[2 * plane, :, lanes] + first * re
                    next_ref[2 * plane + 1, :, lanes] = later_ref[2 * plane + 1, :, lanes] + first * im
            lines = eight(response, 1.0)
            for j in range(8):
                re, im = twisted(lines[j], twist_ref, j, 1)
                rows = pl.ds(member * 64 + j * 8, 8)
                re_ref[rows, :] = re
                im_ref[rows, :] = im
        to_peers(o_ref, pair, matrix, re_ref, im_ref, 6)


def turn_kernel(x_ref, early_ref, mx_ref, twist_ref, traction_ref, o_ref, re_ref, im_ref, plane_ref):
    matrix = (mx_ref[0], mx_ref[1])

    def put(plane, tile, value):
        traction_ref[tile, pl.ds(plane * 8, 8), :] = value
        gain = early_ref[tile, pl.ds(48 + (plane // 3) * 8, 8), :]
        plane_ref[tile, pl.ds(plane * 8, 8), :] = early_ref[tile, pl.ds(plane * 8, 8), :] + gain * value

    strike_inverse(x_ref, twist_ref, matrix, re_ref, im_ref, put)
    take = lambda plane, tile: plane_ref[tile, pl.ds(plane * 8, 8), :]
    strike_forward(take, twist_ref, matrix, o_ref, re_ref, im_ref)


def inverse_kernel(x_ref, mx_ref, twist_ref, traction_ref, re_ref, im_ref):
    matrix = (mx_ref[0], mx_ref[1])

    def put(plane, tile, value):
        traction_ref[tile, pl.ds(plane * 8, 8), :] = value

    strike_inverse(x_ref, twist_ref, matrix, re_ref, im_ref, put)


def history_kernel(history_ref, memory_ref, now_ref, next_ref):
    lags = history_ref.shape[2]
    for tile in range(8):
        lanes = pl.ds(tile * PEERS, PEERS)
        for part in range(2):
            now = jnp.zeros((8, PEERS), f32)
            later = jnp.zeros((8, PEERS), f32)
            for lag in range(lags):
                value = history_ref[0, 0, lag, part, :, lanes]
                now = now + memory_ref[0, lag, :, lanes] * value
                if lag + 1 < lags:
                    later = later + memory_ref[0, lag + 1, :, lanes] * value
            now_ref[0, 0, part, :, lanes] = now
            next_ref[0, 0, part, :, lanes] = later


def planes_kernel(low_ref, high_ref, o_ref):
    for plane in range(6):
        source = low_ref if plane < 3 else high_ref
        for tile in range(GX):
            o_ref[tile, pl.ds(plane * 8, 8), :] = source[plane % 3, 0, pl.ds(tile * 8, 8), :]


def lane_index(shape):
    return lax.broadcasted_iota(jnp.int32, shape, len(shape) - 1)


def packed_column(values, column, lane):
    out = jnp.zeros(values[0].shape, f32)
    for k, value in enumerate(values):
        shift = (k - column) % PEERS
        moved = pltpu.roll(value, shift, 1) if shift else value
        out = jnp.where(lane == k, moved, out)
    return out


def zones_kernel(table_ref, zones_ref, x_ref, y_ref, coef_ref, west_ref, south_ref):
    for z in range(4):
        zone = zones_ref[z]
        rows = [jnp.zeros(zone.shape, f32)] * 3
        for index in range(table_ref.shape[1]):
            matched = zone == index
            rows = [jnp.where(matched, table_ref[row, index], rows[row]) for row in range(3)]
        coef_ref[0, z] = rows[0] * time_step
        coef_ref[1, z] = rows[1] * time_step
        coef_ref[2, z] = rows[2]
    lane = lane_index((64, PEERS))
    west_ref[...] = packed_column([x_ref[k // 4, 0, k % 4] for k in range(12)], PEERS - 1, lane)
    for k in range(12):
        south_ref[pl.ds(k, 1), :] = y_ref[k // 4, 0, k % 4, pl.ds(7, 1), :]


def early_kernel(feed, velocity_ref, stress_ref, west_ref, south_ref, coef_ref, early_ref, *feed_refs):
    lane = lane_index((64, PEERS))
    row = lax.broadcasted_iota(jnp.int32, (64, PEERS), 0)
    west = west_ref[...]
    for c in range(3):
        for z in range(4):
            k = c * 4 + z
            x, y = stress_ref[c, 0, z], stress_ref[c, 1, z]
            edge = pltpu.roll(west, (PEERS - k) % PEERS, 1) if k else west
            behind_x = jnp.where(lane == 0, edge, pltpu.roll(x, 1, 1))
            behind_y = jnp.where(row == 0, south_ref[pl.ds(k, 1), :], pltpu.roll(y, 1, 0))
            force = x - behind_x + y - behind_y
            if z < 3:
                force = force + stress_ref[c, 2, z]
            if z > 0:
                force = force - stress_ref[c, 2, z - 1]
            early = velocity_ref[c, z] + coef_ref[1, z] * force
            early_ref[c, z] = early
            if feed and z in (0, 3):
                plane = c if z == 0 else 3 + c
                for tile in range(GX):
                    feed_refs[0][tile, pl.ds(plane * 8, 8), :] = early[tile * 8 : tile * 8 + 8]
    if feed:
        for tile in range(GX):
            rows = pl.ds(tile * 8, 8)
            feed_refs[0][tile, pl.ds(48, 8), :] = -coef_ref[1, 0, rows, :]
            feed_refs[0][tile, pl.ds(56, 8), :] = coef_ref[1, 3, rows, :]


def velocity_kernel(early_ref, traction_ref, coef_ref, velocity_ref, east_ref, north_ref):
    for c in range(3):
        for z in range(4):
            if z in (1, 2):
                velocity_ref[c, z] = early_ref[c, z]
                continue
            plane = c if z == 0 else 3 + c
            for tile in range(GX):
                rows = pl.ds(tile * 8, 8)
                push = coef_ref[1, z, rows, :] * traction_ref[tile, pl.ds(plane * 8, 8), :]
                base = early_ref[c, z, rows, :]
                velocity_ref[c, z, rows, :] = base - push if z == 0 else base + push
    lane = lane_index((64, PEERS))
    east_ref[...] = packed_column([velocity_ref[k // 4, k % 4] for k in range(12)], 0, lane)
    for k in range(12):
        north_ref[pl.ds(k, 1), :] = velocity_ref[k // 4, k % 4, pl.ds(0, 1), :]


def stress_kernel(rims, velocity_ref, east_ref, north_ref, stress_ref, mask_ref, coef_ref, traction_ref, o_ref, *rim_refs):
    lane = lane_index((64, PEERS))
    row = lax.broadcasted_iota(jnp.int32, (64, PEERS), 0)
    east = east_ref[...]
    for z in range(4):
        rigidity = coef_ref[0, z]
        cohesion = coef_ref[2, z]
        keep = [mask_ref[d, z].astype(f32) for d in range(3)]
        total = jnp.zeros((64, PEERS), f32)
        trial = []
        for c in range(3):
            k = c * 4 + z
            v = velocity_ref[c, z]
            edge = pltpu.roll(east, PEERS - 1 - k, 1)
            ahead_x = jnp.where(lane == PEERS - 1, edge, pltpu.roll(v, PEERS - 1, 1))
            ahead_y = jnp.where(row == 63, north_ref[pl.ds(k, 1), :], pltpu.roll(v, 63, 0))
            tx = keep[0] * (stress_ref[c, 0, z] + rigidity * (ahead_x - v))
            ty = keep[1] * (stress_ref[c, 1, z] + rigidity * (ahead_y - v))
            if z < 3:
                tz = keep[2] * (stress_ref[c, 2, z] + rigidity * (velocity_ref[c, z + 1] - v))
            else:
                pulled = [traction_ref[tile, pl.ds((3 + c) * 8, 8), :] for tile in range(GX)]
                tz = keep[2] * jnp.concatenate(pulled, axis=0)
            trial.append((tx, ty, tz))
            total = total + (tx * tx + ty * ty + tz * tz)
        factor = cohesion / jnp.maximum(jnp.sqrt(total), cohesion)
        for c in range(3):
            for d in range(3):
                o_ref[c, d, z] = trial[c][d] * factor
    if rims:
        west_ref, south_ref = rim_refs
        west_ref[...] = packed_column([o_ref[k // 4, 0, k % 4] for k in range(12)], PEERS - 1, lane)
        for k in range(12):
            south_ref[pl.ds(k, 1), :] = o_ref[k // 4, 1, k % 4, pl.ds(63, 1), :]


def shape(*dims):
    return jax.ShapeDtypeStruct(dims, f32)


WORK = [pltpu.VMEM((PEERS, PEERS), f32), pltpu.VMEM((PEERS, PEERS), f32)]


def call(kernel, outs, *args, scratch=(), name=None):
    return pl.pallas_call(kernel, out_shape=outs, scratch_shapes=list(scratch), name=name)(*args)


def exchange_all(value):
    tiles = value.shape[0] // PEERS
    blocks = value.reshape(PEERS, 1, tiles * PEERS)
    blocks = lax.all_to_all(blocks, both, split_axis=0, concat_axis=0, tiled=True)
    return blocks.reshape(tiles * PEERS, PEERS)


def exchange_row(value):
    return lax.all_to_all(value, "gx", split_axis=0, concat_axis=0, tiled=True)


def shifted(value, axis, steps):
    count = lax.axis_size(axis)
    return lax.ppermute(value, axis, [(source, (source + steps) % count) for source in range(count)])


def planes_of(velocity):
    block = (3, 1, 64, PEERS)
    return pl.pallas_call(
        planes_kernel,
        grid=(1,),
        in_specs=[
            pl.BlockSpec(block, lambda i: (0, 0, 0, 0)),
            pl.BlockSpec(block, lambda i: (0, 3, 0, 0)),
        ],
        out_specs=pl.BlockSpec((GX, 48, PEERS), lambda i: (0, 0, 0)),
        out_shape=shape(GX, 48, PEERS),
        name="planes",
    )(velocity, velocity)


def zones_of(zone_table, zones, stress):
    whole = lambda *dims: pl.BlockSpec(dims, lambda i: (0,) * len(dims))
    return pl.pallas_call(
        zones_kernel,
        grid=(1,),
        in_specs=[
            pl.BlockSpec(memory_space=pltpu.SMEM),
            whole(4, 64, PEERS),
            pl.BlockSpec((3, 1, 4, 64, PEERS), lambda i: (0, 0, 0, 0, 0)),
            pl.BlockSpec((3, 1, 4, 8, PEERS), lambda i: (0, 1, 0, 7, 0)),
        ],
        out_specs=[whole(3, 4, 64, PEERS), whole(64, PEERS), whole(16, PEERS)],
        out_shape=[shape(3, 4, 64, PEERS), shape(64, PEERS), shape(16, PEERS)],
        name="zones",
    )(zone_table, zones, stress, stress)


def tails_of(history, memory):
    out_spec = pl.BlockSpec((1, 1, 2, 8, 1024), lambda p, c: (p, c, 0, 0, 0))
    now, later = pl.pallas_call(
        history_kernel,
        grid=(2, 3),
        in_specs=[
            pl.BlockSpec((1, 1, 31, 2, 8, 1024), lambda p, c: (p, c, 0, 0, 0, 0)),
            pl.BlockSpec((1, 31, 8, 1024), lambda p, c: (p, 0, 0, 0)),
        ],
        out_specs=[out_spec, out_spec],
        out_shape=[shape(2, 3, 2, 8, 1024)] * 2,
        name="tails",
    )(history, memory)
    return now.reshape(12, 8, 1024), later.reshape(12, 8, 1024)


def body(velocity, stress, face_mask, zones, zone_table, impedance, memory, history):
    mx, my, twist = tables()
    impedance = impedance.reshape(6, 8, 1024)
    first = memory[:, 0]
    field = shape(3, 4, 64, PEERS)
    rim_x, rim_y = shape(64, PEERS), shape(16, PEERS)
    packed = shape(6 * PEERS, PEERS)

    rows = exchange_row(planes_of(velocity))
    coef, west, south = zones_of(zone_table, zones, stress)
    west, south = shifted(west, "gx", 1), shifted(south, "gy", 1)
    now, later = tails_of(history, memory)
    sent = exchange_all(call(forward_kernel, packed, rows, mx, twist, scratch=WORK, name="forward"))
    early, feed = call(
        functools.partial(early_kernel, True),
        [field, shape(GX, 64, PEERS)],
        velocity, stress, west, south, coef,
        name="early0",
    )
    feed = exchange_row(feed)
    lines, later = call(
        functools.partial(dip_kernel, True),
        [packed, shape(12, 8, 1024)],
        sent, impedance, now, first, later, my, twist,
        scratch=WORK, name="dip0",
    )
    lines = exchange_all(lines)
    traction, packed_next = call(
        turn_kernel,
        [shape(GX, 48, PEERS), packed],
        lines, feed, mx, twist,
        scratch=WORK + [pltpu.VMEM((GX, 48, PEERS), f32)], name="turn",
    )
    sent = exchange_all(packed_next)
    traction = exchange_row(traction)
    velocity, east, north = call(velocity_kernel, [field, rim_x, rim_y], early, traction, coef, name="velocity0")
    east, north = shifted(east, "gx", -1), shifted(north, "gy", -1)
    lines = call(
        functools.partial(dip_kernel, False), packed, sent, impedance, later, my, twist, scratch=WORK, name="dip1"
    )
    lines = exchange_all(lines)
    stress, west, south = call(
        functools.partial(stress_kernel, True),
        [shape(3, 3, 4, 64, PEERS), rim_x, rim_y],
        velocity, east, north, stress, face_mask, coef, traction,
        name="stress0",
    )
    west, south = shifted(west, "gx", 1), shifted(south, "gy", 1)
    early = call(
        functools.partial(early_kernel, False), field, velocity, stress, west, south, coef, name="early1"
    )
    traction = call(inverse_kernel, shape(GX, 48, PEERS), lines, mx, twist, scratch=WORK, name="inverse")
    traction = exchange_row(traction)
    velocity, east, north = call(velocity_kernel, [field, rim_x, rim_y], early, traction, coef, name="velocity1")
    east, north = shifted(east, "gx", -1), shifted(north, "gy", -1)
    stress = call(
        functools.partial(stress_kernel, False),
        shape(3, 3, 4, 64, PEERS),
        velocity, east, north, stress, face_mask, coef, traction,
        name="stress1",
    )
    return (velocity, stress)


def solution(mesh):
    in_specs = (
        P(None, None, "gy", "gx"),
        P(None, None, None, "gy", "gx"),
        P(None, None, "gy", "gx"),
        P(None, "gy", "gx"),
        P(),
        P(None, None, both, None),
        P(None, None, both, None),
        P(None, None, None, None, both, None),
    )
    out_specs = (P(None, None, "gy", "gx"), P(None, None, None, "gy", "gx"))
    return jax.shard_map(body, mesh=mesh, in_specs=in_specs, out_specs=out_specs, check_vma=False)
```

```python
import functools
import math

import jax
import jax.numpy as jnp
import numpy as np
from jax import lax
from jax.experimental import pallas as pl
from jax.experimental.pallas import tpu as pltpu
from jax.sharding import PartitionSpec as P


time_step = 0.2
GX = 8
GY = 16
PEERS = 128
f32 = jnp.float32
bf16 = jnp.bfloat16
TILES = 7
both = ("gx", "gy")
half_root = math.sqrt(0.5)


def halves(table):
    high = jnp.asarray(table, f32).astype(bf16)
    low = (jnp.asarray(table, f32) - high.astype(f32)).astype(bf16)
    return jnp.stack([high, low])


def tables():
    index = np.arange(PEERS)
    angle = 2.0 * np.pi * (np.outer(index, index) % PEERS) / PEERS
    c, s = np.cos(angle) / 32.0, np.sin(angle) / 32.0
    along_x = np.block([[c, s], [-s, c]])
    place = 8 * (index % GY) + index // GY
    angle = 2.0 * np.pi * (np.outer(place, index) % PEERS) / PEERS
    c, s = np.cos(angle) / 32.0, np.sin(angle) / 32.0
    along_y = np.block([[c, -s], [s, c]])
    turn = 2.0 * np.pi * np.outer(np.arange(8), index) / 1024.0
    twist = np.stack([np.cos(turn), np.sin(turn)])
    twist = np.broadcast_to(twist[:, :, None, :], (2, 8, 8, PEERS))
    turn = 2.0 * np.pi * index / PEERS
    ahead = np.broadcast_to(np.stack([np.cos(turn), np.sin(turn)])[:, None, :], (2, 8, PEERS))
    return halves(along_x), halves(along_y), jnp.asarray(twist, f32), jnp.asarray(ahead, f32)


def plus(a, b):
    imag = a[1] if b[1] is None else b[1] if a[1] is None else a[1] + b[1]
    return (a[0] + b[0], imag)


def minus(a, b):
    imag = a[1] if b[1] is None else -b[1] if a[1] is None else a[1] - b[1]
    return (a[0] - b[0], imag)


def turned(a, sign):
    if a[1] is None:
        return (jnp.zeros_like(a[0]), a[0] if sign > 0 else -a[0])
    return (-a[1], a[0]) if sign > 0 else (a[1], -a[0])


def four(x, sign):
    a, b = plus(x[0], x[2]), minus(x[0], x[2])
    c, d = plus(x[1], x[3]), turned(minus(x[1], x[3]), sign)
    return [plus(a, c), plus(b, d), minus(a, c), minus(b, d)]


def eight(x, sign):
    even, odd = four(x[0::2], sign), four(x[1::2], sign)
    o1, o3 = odd[1], odd[3]
    odd1 = ((o1[0] - sign * o1[1]) * half_root, (o1[1] + sign * o1[0]) * half_root)
    odd3 = ((-o3[0] - sign * o3[1]) * half_root, (sign * o3[0] - o3[1]) * half_root)
    odd = [odd[0], odd1, turned(odd[2], sign), odd3]
    return [plus(e, o) for e, o in zip(even, odd)] + [minus(e, o) for e, o in zip(even, odd)]


def split(x):
    high = x.astype(bf16)
    return high, (x - high.astype(f32)).astype(bf16)


def product(a, b, dims):
    dot = functools.partial(lax.dot_general, dimension_numbers=(dims, ((), ())), preferred_element_type=f32)
    return dot(a[0], b[0]) + (dot(a[1], b[0]) + dot(a[0], b[1]))


def from_peers(x_ref, pair, matrix, re_ref, im_ref, tiles):
    x = jnp.concatenate([x_ref[pl.ds(2 * pair + part, PEERS, stride=tiles), :] for part in range(2)], axis=0)
    y = product(split(x), matrix, ((0,), (0,)))
    re_ref[...] = y[:, :PEERS]
    im_ref[...] = y[:, PEERS:]


def to_peers(o_ref, pair, matrix, re_ref, im_ref, tiles):
    t = split(jnp.concatenate([re_ref[...], im_ref[...]], axis=1))
    out = product(matrix, t, ((1,), (1,)))
    for part in range(2):
        o_ref[pl.ds(2 * pair + part, PEERS, stride=tiles), :] = out[part * PEERS : (part + 1) * PEERS]


def twisted(value, twist_ref, index, sign):
    if index == 0:
        return value
    c, s = twist_ref[0, index], twist_ref[1, index]
    if sign < 0:
        return (value[0] * c + value[1] * s, value[1] * c - value[0] * s)
    return (value[0] * c - value[1] * s, value[1] * c + value[0] * s)


def strike_forward(take, twist_ref, matrix, o_ref, re_ref, im_ref):
    for pair in range(3):
        for member in range(2):
            plane = 2 * pair + member
            waves = eight([(take(plane, tile), None) for tile in range(GX)], -1.0)
            for k in range(8):
                re, im = waves[k]
                if im is None:
                    im = jnp.zeros_like(re)
                re, im = twisted((re, im), twist_ref, k, -1)
                rows = pl.ds(member * 64 + k * 8, 8)
                re_ref[rows, :] = re
                im_ref[rows, :] = im
        to_peers(o_ref, pair, matrix, re_ref, im_ref, 6)


def strike_inverse(x_ref, twist_ref, matrix, d_ref, re_ref, im_ref, put):
    lane = lane_index((8, PEERS))
    edges = [jnp.zeros((8, PEERS), f32)] * GX
    for pair in range(3):
        from_peers(x_ref, pair, matrix, re_ref, im_ref, TILES)
        for member in range(2):
            plane = 2 * pair + member
            values = []
            for k in range(8):
                rows = pl.ds(member * 64 + k, 8, stride=8)
                values.append(twisted((re_ref[rows, :], im_ref[rows, :]), twist_ref, k, 1))
            field = eight(values, 1.0)
            for tile in range(GX):
                value = field[tile][0]
                d_ref[tile, pl.ds(plane * 8, 8), :] = value
                moved = pltpu.roll(value, plane, 1) if plane else value
                before = (tile + GX - 1) % GX
                edges[before] = jnp.where(lane == plane, moved, edges[before])
                put(plane, tile, value)
    for tile in range(GX):
        d_ref[tile, pl.ds(56, 8), :] = edges[tile]
    x = split(x_ref[pl.ds(6, PEERS, stride=TILES), :])
    y = product(x, (matrix[0][:PEERS], matrix[1][:PEERS]), ((0,), (0,)))
    re_ref[...] = y[:, :PEERS]
    im_ref[...] = y[:, PEERS:]
    values = []
    for k in range(8):
        low, high = pl.ds(k, 8, stride=8), pl.ds(64 + k, 8, stride=8)
        value = (re_ref[low, :] - im_ref[high, :], im_ref[low, :] + re_ref[high, :])
        values.append(twisted(value, twist_ref, k, 1))
    field = eight(values, 1.0)
    for tile in range(GX):
        d_ref[tile, pl.ds(48, 8), :] = field[tile][0]


def forward_kernel(x_ref, mx_ref, twist_ref, o_ref, re_ref, im_ref):
    matrix = (mx_ref[0], mx_ref[1])
    take = lambda plane, tile: x_ref[tile, pl.ds(plane * 24, 8), :]
    strike_forward(take, twist_ref, matrix, o_ref, re_ref, im_ref)


def dip_kernel(carry, x_ref, my_ref, twist_ref, ahead_ref, impedance_ref, *refs):
    if carry:
        now, (memory_ref, *later) = refs[:2], refs[2:5]
        o_ref, *next_refs = refs[5:8]
        re_ref, im_ref, re2_ref, im2_ref, z_ref, tail_ref, sems, first_ref, later_ref, more_sems = refs[8:]
    else:
        now = refs[:2]
        o_ref, re_ref, im_ref, re2_ref, im2_ref, z_ref, tail_ref, sems = refs[2:]

    def copies(pair):
        jobs = []
        for plane in (2 * pair, 2 * pair + 1):
            side, part = plane // 3, pl.ds(2 * (plane % 3), 2)
            jobs.append((impedance_ref.at[plane], z_ref.at[plane], sems.at[plane, 0]))
            jobs.append((now[side].at[part], tail_ref.at[plane], sems.at[plane, 1]))
            if carry:
                jobs.append((later[side].at[part], later_ref.at[plane], more_sems.at[plane, 0]))
        if carry and pair == 0:
            jobs.append((memory_ref.at[:, 0], first_ref, more_sems.at[6, 0]))
        return [pltpu.make_async_copy(*job) for job in jobs]

    arriving = [copies(pair) for pair in range(3)]
    for group in arriving:
        for copy in group:
            copy.start()
    leaving = []
    matrix = (my_ref[0], my_ref[1])
    re2_ref[...] = jnp.zeros((PEERS, PEERS), f32)
    im2_ref[...] = jnp.zeros((PEERS, PEERS), f32)
    c8, s8 = ahead_ref[0], ahead_ref[1]
    for pair in range(3):
        from_peers(x_ref, pair, matrix, re_ref, im_ref, 6)
        for copy in arriving[pair]:
            copy.wait()
        for member in range(2):
            plane = 2 * pair + member
            side, part = plane // 3, 2 * (plane % 3)
            values = []
            for j in range(8):
                rows = pl.ds(member * 64 + j, 8, stride=8)
                values.append(twisted((re_ref[rows, :], im_ref[rows, :]), twist_ref, j, -1))
            spectrum = eight(values, -1.0)
            response = []
            for tile in range(8):
                lanes = pl.ds(tile * PEERS, PEERS)
                z = z_ref[plane, :, lanes]
                re, im = spectrum[tile]
                response.append((tail_ref[plane, 0, :, lanes] - z * re, tail_ref[plane, 1, :, lanes] - z * im))
                if carry:
                    first = first_ref[side, :, lanes]
                    later_ref[plane, 0, :, lanes] = later_ref[plane, 0, :, lanes] + first * re
                    later_ref[plane, 1, :, lanes] = later_ref[plane, 1, :, lanes] + first * im
            if carry:
                target = next_refs[side].at[pl.ds(part, 2)]
                leaving.append(pltpu.make_async_copy(later_ref.at[plane], target, more_sems.at[plane, 1]))
                leaving[-1].start()
            lines = eight(response, 1.0)
            for j in range(8):
                re, im = twisted(lines[j], twist_ref, j, 1)
                rows = pl.ds(member * 64 + j * 8, 8)
                re_ref[rows, :] = re
                im_ref[rows, :] = im
                if j == 0:
                    re, im = re * c8 - im * s8, im * c8 + re * s8
                    for half, (a, b) in enumerate(((re, im), (im, -re))):
                        rows = pl.ds(half * 64 + plane * 8, 8)
                        re2_ref[rows, :] = a
                        im2_ref[rows, :] = b
        to_peers(o_ref, pair, matrix, re_ref, im_ref, TILES)
    t = split(jnp.concatenate([re2_ref[...], im2_ref[...]], axis=1))
    o_ref[pl.ds(6, PEERS, stride=TILES), :] = product((matrix[0][:PEERS], matrix[1][:PEERS]), t, ((1,), (1,)))
    for copy in leaving:
        copy.wait()


def turn_kernel(x_ref, early_ref, mx_ref, twist_ref, o_ref, d_ref, re_ref, im_ref, plane_ref):
    matrix = (mx_ref[0], mx_ref[1])

    def put(plane, tile, value):
        gain = early_ref[tile, pl.ds(48 + (plane // 3) * 8, 8), :]
        plane_ref[tile, pl.ds(plane * 8, 8), :] = early_ref[tile, pl.ds(plane * 8, 8), :] + gain * value

    strike_inverse(x_ref, twist_ref, matrix, d_ref, re_ref, im_ref, put)
    take = lambda plane, tile: plane_ref[tile, pl.ds(plane * 8, 8), :]
    strike_forward(take, twist_ref, matrix, o_ref, re_ref, im_ref)


def inverse_kernel(x_ref, mx_ref, twist_ref, d_ref, re_ref, im_ref):
    matrix = (mx_ref[0], mx_ref[1])
    strike_inverse(x_ref, twist_ref, matrix, d_ref, re_ref, im_ref, lambda plane, tile, value: None)


def history_kernel(history_ref, memory_ref, now_ref, next_ref):
    lags = history_ref.shape[2]
    for tile in range(8):
        lanes = pl.ds(tile * PEERS, PEERS)
        for part in range(2):
            now = jnp.zeros((8, PEERS), f32)
            later = jnp.zeros((8, PEERS), f32)
            for lag in range(lags):
                value = history_ref[0, 0, lag, part, :, lanes]
                now = now + memory_ref[0, lag, :, lanes] * value
                if lag + 1 < lags:
                    later = later + memory_ref[0, lag + 1, :, lanes] * value
            now_ref[part, :, lanes] = now
            next_ref[part, :, lanes] = later


def pack_kernel(table_ref, velocity_ref, stress_ref, zones_ref, o_ref, v_ref, x_ref, y_ref, z_ref, zone_ref, sems):
    copies = []
    for side in range(2):
        jobs = (
            (velocity_ref.at[:, 3 * side], v_ref.at[side]),
            (stress_ref.at[:, 0, 3 * side], x_ref.at[side]),
            (stress_ref.at[:, 1, 3 * side], y_ref.at[side]),
            (stress_ref.at[:, 2, 2 * side], z_ref.at[side]),
            (zones_ref.at[3 * side], zone_ref.at[side]),
        )
        for number, (source, target) in enumerate(jobs):
            copies.append(pltpu.make_async_copy(source, target, sems.at[side, number]))
    for copy in copies:
        copy.start()
    for copy in copies:
        copy.wait()
    row = lax.broadcasted_iota(jnp.int32, (64, PEERS), 0)
    for side in range(2):
        zone = zone_ref[side]
        gain = jnp.zeros(zone.shape, f32)
        for index in range(table_ref.shape[1]):
            gain = jnp.where(zone == index, table_ref[1, index], gain)
        gain = gain * time_step
        for c in range(3):
            plane = 3 * side + c
            v, x, y, z = v_ref[side, c], x_ref[side, c], y_ref[side, c], z_ref[side, c]
            behind = jnp.where(row == 0, 0.0, pltpu.roll(y, 1, 0))
            force = x + (y - behind) + (z if side == 0 else -z)
            early = v + gain * force
            for tile in range(GX):
                lines = slice(tile * 8, tile * 8 + 8)
                o_ref[tile, pl.ds(plane * 24, 8), :] = v[lines]
                o_ref[tile, pl.ds(plane * 24 + 8, 8), :] = early[lines]
                o_ref[tile, pl.ds(plane * 24 + 16, 8), :] = x[lines]
                o_ref[tile, pl.ds(160 + plane, 1), :] = y_ref[side, c, pl.ds(63, 1), :]
        for tile in range(GX):
            signed = gain[tile * 8 : tile * 8 + 8]
            o_ref[tile, pl.ds(144 + 8 * side, 8), :] = -signed if side == 0 else signed
            o_ref[tile, pl.ds(166 + side, 1), :] = jnp.zeros((1, PEERS), f32)


def lane_index(shape):
    return lax.broadcasted_iota(jnp.int32, shape, len(shape) - 1)


def packed_column(values, column, lane):
    out = jnp.zeros(values[0].shape, f32)
    for k, value in enumerate(values):
        shift = (k - column) % PEERS
        moved = pltpu.roll(value, shift, 1) if shift else value
        out = jnp.where(lane == k, moved, out)
    return out


def zones_kernel(table_ref, zones_ref, x_ref, y_ref, coef_ref, west_ref, south_ref):
    for z in range(4):
        zone = zones_ref[z]
        rows = [jnp.zeros(zone.shape, f32)] * 3
        for index in range(table_ref.shape[1]):
            matched = zone == index
            rows = [jnp.where(matched, table_ref[row, index], rows[row]) for row in range(3)]
        coef_ref[0, z] = rows[0] * time_step
        coef_ref[1, z] = rows[1] * time_step
        coef_ref[2, z] = rows[2]
    lane = lane_index((64, PEERS))
    west_ref[...] = packed_column([x_ref[k // 4, 0, k % 4] for k in range(12)], PEERS - 1, lane)
    for k in range(12):
        south_ref[pl.ds(k, 1), :] = y_ref[k // 4, 0, k % 4, pl.ds(7, 1), :]


def pushed(c, z, lane, row, velocity, stress_ref, west, south_ref, gain):
    k = c * 4 + z
    x, y = stress_ref[c, 0, z], stress_ref[c, 1, z]
    edge = pltpu.roll(west, PEERS - k, 1) if k else west
    behind_x = jnp.where(lane == 0, edge, pltpu.roll(x, 1, 1))
    behind_y = jnp.where(row == 0, south_ref[pl.ds(k, 1), :], pltpu.roll(y, 1, 0))
    force = x - behind_x + y - behind_y
    if z < 3:
        force = force + stress_ref[c, 2, z]
    if z > 0:
        force = force - stress_ref[c, 2, z - 1]
    return velocity + gain * force


def early_kernel(velocity_ref, stress_ref, west_ref, south_ref, coef_ref, mark_ref, early_ref, east_ref, north_ref):
    lane = lane_index((64, PEERS))
    row = lax.broadcasted_iota(jnp.int32, (64, PEERS), 0)
    west = west_ref[...]
    for c in range(3):
        for z in range(4):
            early_ref[c, z] = pushed(
                c, z, lane, row, velocity_ref[c, z], stress_ref, west, south_ref, coef_ref[1, z]
            )
    fields = [early_ref.at[k // 4, k % 4] for k in range(12)] + [coef_ref.at[1, 0], coef_ref.at[1, 3]]
    east_ref[...] = packed_column([field[...] for field in fields], 0, lane)
    for k, field in enumerate(fields):
        north_ref[pl.ds(k, 1), :] = field[pl.ds(0, 1), :]
    north_ref[pl.ds(14, 2), :] = jnp.zeros((2, PEERS), f32)


def feed_kernel(rows_ref, south_ref, feed_ref):
    lane = lane_index((8, PEERS))
    row = lax.broadcasted_iota(jnp.int32, (8, PEERS), 0)
    for tile in range(GX):
        for side in range(2):
            signed = rows_ref[tile, pl.ds(144 + 8 * side, 8), :]
            feed_ref[tile, pl.ds(48 + 8 * side, 8), :] = signed
            gain = -signed if side == 0 else signed
            for c in range(3):
                plane = 3 * side + c
                lines = pl.ds(plane * 24 + 16, 8)
                x, before = rows_ref[tile, lines, :], rows_ref[(tile + GX - 1) % GX, lines, :]
                behind = jnp.where(lane == 0, pltpu.roll(before, 1, 1), pltpu.roll(x, 1, 1))
                south = jnp.where(row == 0, south_ref[tile, pl.ds(plane, 1), :], 0.0)
                early = rows_ref[tile, pl.ds(plane * 24 + 8, 8), :]
                feed_ref[tile, pl.ds(plane * 8, 8), :] = early - gain * (behind + south)


def cells_kernel(rims, early_ref, east_ref, north_ref, d_ref, coef_ref, stress_ref, mask_ref, v_ref, o_ref, *refs):
    lane = lane_index((64, PEERS))
    row = lax.broadcasted_iota(jnp.int32, (64, PEERS), 0)
    for c in range(3):
        for z in range(4):
            v_ref[c, z] = early_ref[c, z]
    for tile in range(GX):
        rows = pl.ds(tile * 8, 8)
        for plane in range(6):
            c, z = plane % 3, 3 * (plane // 3)
            push = coef_ref[1, z, rows, :] * d_ref[tile, pl.ds(plane * 8, 8), :]
            base = early_ref[c, z, rows, :]
            v_ref[c, z, rows, :] = base - push if z == 0 else base + push
    east = east_ref[...]
    edge = jnp.concatenate([d_ref[tile, pl.ds(56, 8), :] for tile in range(GX)], axis=0)
    last = lambda value, k: pltpu.roll(value, PEERS - 1 - k, 1)
    for z in range(4):
        rigidity = coef_ref[0, z]
        cohesion = coef_ref[2, z]
        keep = [mask_ref[d, z].astype(f32) for d in range(3)]
        total = jnp.zeros((64, PEERS), f32)
        trial = []
        for c in range(3):
            k = c * 4 + z
            v = v_ref[c, z]
            past_x, past_y = last(east, k), north_ref[pl.ds(k, 1), :]
            if z in (0, 3):
                plane, gain = c + z, 12 if z == 0 else 13
                push_x = last(east, gain) * last(edge, plane)
                push_y = north_ref[pl.ds(gain, 1), :] * d_ref[GX - 1, pl.ds(48 + plane, 1), :]
                past_x = past_x - push_x if z == 0 else past_x + push_x
                past_y = past_y - push_y if z == 0 else past_y + push_y
            ahead_x = jnp.where(lane == PEERS - 1, past_x, pltpu.roll(v, PEERS - 1, 1))
            ahead_y = jnp.where(row == 63, past_y, pltpu.roll(v, 63, 0))
            tx = keep[0] * (stress_ref[c, 0, z] + rigidity * (ahead_x - v))
            ty = keep[1] * (stress_ref[c, 1, z] + rigidity * (ahead_y - v))
            if z < 3:
                tz = keep[2] * (stress_ref[c, 2, z] + rigidity * (v_ref[c, z + 1] - v))
            else:
                pulled = [d_ref[tile, pl.ds((3 + c) * 8, 8), :] for tile in range(GX)]
                tz = keep[2] * jnp.concatenate(pulled, axis=0)
            trial.append((tx, ty, tz))
            total = total + (tx * tx + ty * ty + tz * tz)
        factor = cohesion / jnp.maximum(jnp.sqrt(total), cohesion)
        for c in range(3):
            for d in range(3):
                o_ref[c, d, z] = trial[c][d] * factor
    if rims:
        west_ref, south_ref = refs
        west_ref[...] = packed_column([o_ref[k // 4, 0, k % 4] for k in range(12)], PEERS - 1, lane)
        for k in range(12):
            south_ref[pl.ds(k, 1), :] = o_ref[k // 4, 1, k % 4, pl.ds(63, 1), :]
        south_ref[pl.ds(12, 4), :] = jnp.zeros((4, PEERS), f32)


def shape(*dims):
    return jax.ShapeDtypeStruct(dims, f32)


WORK = [pltpu.VMEM((PEERS, PEERS), f32), pltpu.VMEM((PEERS, PEERS), f32)]


def near(*dims):
    return pltpu.VMEM(dims, f32)


def room(size):
    return pltpu.CompilerParams(vmem_limit_bytes=size << 20)


def far(*dims):
    return pltpu.HBM(dims, f32)


def held(arrays, space):
    return [pltpu.with_memory_space_constraint(a, space) for a in arrays]


def call(kernel, outs, *args, scratch=(), close=True):
    args = held(args, pltpu.VMEM if close else pltpu.HBM)
    return pl.pallas_call(kernel, out_shape=outs, scratch_shapes=list(scratch), compiler_params=room(8))(*args)


def exchange_all(value):
    tiles = value.shape[0] // PEERS
    blocks = value.reshape(PEERS, 1, tiles * PEERS)
    blocks = lax.all_to_all(blocks, both, split_axis=0, concat_axis=0, tiled=True)
    return blocks.reshape(tiles * PEERS, PEERS)


def exchange_row(value):
    return lax.all_to_all(value, "gx", split_axis=0, concat_axis=0, tiled=True)


def shifted(value, axis, steps):
    count = lax.axis_size(axis)
    return lax.ppermute(value, axis, [(source, (source + steps) % count) for source in range(count)])


def pack(zone_table, velocity, stress, zones):
    whole = pl.BlockSpec(memory_space=pltpu.HBM)
    field = pltpu.VMEM((2, 3, 64, PEERS), f32)
    return pl.pallas_call(
        pack_kernel,
        in_specs=[pl.BlockSpec(memory_space=pltpu.SMEM), whole, whole, whole],
        out_shape=near(GX, 168, PEERS),
        scratch_shapes=[field] * 4 + [pltpu.VMEM((2, 64, PEERS), jnp.int32), pltpu.SemaphoreType.DMA((2, 5))],
        compiler_params=room(16),
        name="pack",
    )(zone_table, *held((velocity, stress, zones), pltpu.HBM))


def zones_of(zone_table, zones, stress):
    whole = lambda *dims: pl.BlockSpec(dims, lambda i: (0,) * len(dims))
    return pl.pallas_call(
        zones_kernel,
        grid=(1,),
        in_specs=[
            pl.BlockSpec(memory_space=pltpu.SMEM),
            whole(4, 64, PEERS),
            pl.BlockSpec((3, 1, 4, 64, PEERS), lambda i: (0, 0, 0, 0, 0)),
            pl.BlockSpec((3, 1, 4, 8, PEERS), lambda i: (0, 1, 0, 7, 0)),
        ],
        out_specs=[whole(3, 4, 64, PEERS), whole(64, PEERS), whole(16, PEERS)],
        out_shape=[far(3, 4, 64, PEERS), far(64, PEERS), far(16, PEERS)],
        compiler_params=room(16),
        name="zones",
    )(zone_table, *held((zones, stress, stress), pltpu.HBM))


def tails_of(history, memory, plane):
    out_spec = pl.BlockSpec((2, 8, 1024), lambda c: (c, 0, 0))
    return pl.pallas_call(
        history_kernel,
        grid=(3,),
        in_specs=[
            pl.BlockSpec((1, 1, 31, 2, 8, 1024), lambda c: (plane, c, 0, 0, 0, 0)),
            pl.BlockSpec((1, 31, 8, 1024), lambda c: (plane, 0, 0, 0)),
        ],
        out_specs=[out_spec, out_spec],
        out_shape=[far(6, 8, 1024)] * 2,
        compiler_params=room(16),
    )(*held((history, memory), pltpu.HBM))


def mark_kernel(x_ref, o_ref):
    o_ref[...] = x_ref[0, 0, pl.ds(0, 8), :]


def steps(velocity, stress, face_mask, zones, zone_table, impedance, memory, history):
    mx, my, twist, ahead = tables()
    impedance = impedance.reshape(6, 8, 1024)
    sending, returning = near(6 * PEERS, PEERS), near(TILES * PEERS, PEERS)
    dma = pltpu.SemaphoreType.DMA
    line = pltpu.VMEM((6, 2, 8, 1024), f32)

    def make_dip(carry, sent, *operands):
        spec = lambda space, count: [pl.BlockSpec(memory_space=space)] * count
        scratch = [square] * 4 + [pltpu.VMEM((6, 8, 1024), f32), line, dma((6, 2))]
        outs, out_specs = returning, spec(pltpu.VMEM, 1)[0]
        if carry:
            scratch += [pltpu.VMEM((2, 8, 1024), f32), line, dma((7, 2))]
            outs = [returning, far(6, 8, 1024), far(6, 8, 1024)]
            out_specs = spec(pltpu.VMEM, 1) + spec(pltpu.HBM, 2)
        return pl.pallas_call(
            functools.partial(dip_kernel, carry),
            in_specs=spec(pltpu.VMEM, 4) + spec(pltpu.HBM, len(operands)),
            out_specs=out_specs,
            out_shape=outs,
            scratch_shapes=scratch,
            compiler_params=room(8),
        )(*held((sent, my, twist, ahead), pltpu.VMEM), *held(operands, pltpu.HBM))

    square = pltpu.VMEM((PEERS, PEERS), f32)

    def make_early(velocity, stress, west, south, mark):
        outs = [far(3, 4, 64, PEERS), far(64, PEERS), far(16, PEERS)]
        return call(early_kernel, outs, velocity, stress, west, south, coef, mark, close=False)

    def make_cells(rims, *operands):
        outs = [shape(3, 4, 64, PEERS), shape(3, 3, 4, 64, PEERS)]
        if rims:
            outs = [far(3, 4, 64, PEERS), far(3, 3, 4, 64, PEERS), far(64, PEERS), far(16, PEERS)]
        return call(functools.partial(cells_kernel, rims), outs, *operands, close=not rims)

    rows = exchange_row(pack(zone_table, velocity, stress, zones))
    coef, west, south = zones_of(zone_table, zones, stress)
    west, south = shifted(west, "gx", 1), shifted(south, "gy", 1)
    now, later = zip(tails_of(history, memory, 0), tails_of(history, memory, 1))
    sent = exchange_all(call(forward_kernel, sending, rows, mx, twist, scratch=WORK))
    onward = [((GX - 1) * GY + h, (h + 1) % GY) for h in range(GY)]
    above = lax.ppermute(rows[:, 160:168], both, onward)
    early, east, north = make_early(velocity, stress, west, south, south)
    east, north = shifted(east, "gx", -1), shifted(north, "gy", -1)
    lines, *later = make_dip(True, sent, impedance, *now, memory, *later)
    lines = exchange_all(lines)
    feed = call(feed_kernel, near(GX, 64, PEERS), rows, above)
    sending1, traction = call(
        turn_kernel,
        [sending, near(GX, 64, PEERS)],
        lines, feed, mx, twist,
        scratch=[square] * 2 + [pltpu.VMEM((GX, 48, PEERS), f32)],
    )
    sent = exchange_all(sending1)
    traction = exchange_row(traction)
    lines = make_dip(False, sent, impedance, *later)
    lines = exchange_all(lines)
    velocity, stress, west, south = make_cells(True, early, east, north, traction, coef, stress, face_mask)
    west, south = shifted(west, "gx", 1), shifted(south, "gy", 1)
    mark = call(mark_kernel, shape(8, PEERS), coef, close=False)
    early, east, north = make_early(velocity, stress, west, south, mark)
    east, north = shifted(east, "gx", -1), shifted(north, "gy", -1)
    traction = call(inverse_kernel, near(GX, 64, PEERS), lines, mx, twist, scratch=[square] * 2)
    traction = exchange_row(traction)
    velocity, stress = make_cells(False, early, east, north, traction, coef, stress, face_mask)
    return (velocity, stress)


def solution(mesh):
    in_specs = (
        P(None, None, "gy", "gx"),
        P(None, None, None, "gy", "gx"),
        P(None, None, "gy", "gx"),
        P(None, "gy", "gx"),
        P(),
        P(None, None, both, None),
        P(None, None, both, None),
        P(None, None, None, None, both, None),
    )
    out_specs = (P(None, None, "gy", "gx"), P(None, None, None, "gy", "gx"))
    return jax.shard_map(steps, mesh=mesh, in_specs=in_specs, out_specs=out_specs, check_vma=False)
```

```python
import functools
import math

import jax
import jax.numpy as jnp
import numpy as np
from jax import lax
from jax.experimental import pallas as pl
from jax.experimental.pallas import tpu as pltpu
from jax.sharding import PartitionSpec as P


time_step = 0.2
GX = 8
GY = 16
PEERS = 128
f32 = jnp.float32
bf16 = jnp.bfloat16
TILES = 7
both = ("gx", "gy")
half_root = math.sqrt(0.5)


def halves(table):
    high = jnp.asarray(table, f32).astype(bf16)
    low = (jnp.asarray(table, f32) - high.astype(f32)).astype(bf16)
    return jnp.stack([high, low])


def tables():
    index = np.arange(PEERS)
    angle = 2.0 * np.pi * (np.outer(index, index) % PEERS) / PEERS
    c, s = np.cos(angle) / 32.0, np.sin(angle) / 32.0
    along_x = np.block([[c, s], [-s, c]])
    place = 8 * (index % GY) + index // GY
    angle = 2.0 * np.pi * (np.outer(place, index) % PEERS) / PEERS
    c, s = np.cos(angle) / 32.0, np.sin(angle) / 32.0
    along_y = np.block([[c, -s], [s, c]])
    turn = 2.0 * np.pi * np.outer(np.arange(8), index) / 1024.0
    twist = np.stack([np.cos(turn), np.sin(turn)])
    twist = np.broadcast_to(twist[:, :, None, :], (2, 8, 8, PEERS))
    turn = 2.0 * np.pi * index / PEERS
    ahead = np.broadcast_to(np.stack([np.cos(turn), np.sin(turn)])[:, None, :], (2, 8, PEERS))
    return halves(along_x), halves(along_y), jnp.asarray(twist, f32), jnp.asarray(ahead, f32)


def plus(a, b):
    imag = a[1] if b[1] is None else b[1] if a[1] is None else a[1] + b[1]
    return (a[0] + b[0], imag)


def minus(a, b):
    imag = a[1] if b[1] is None else -b[1] if a[1] is None else a[1] - b[1]
    return (a[0] - b[0], imag)


def turned(a, sign):
    if a[1] is None:
        return (jnp.zeros_like(a[0]), a[0] if sign > 0 else -a[0])
    return (-a[1], a[0]) if sign > 0 else (a[1], -a[0])


def four(x, sign):
    a, b = plus(x[0], x[2]), minus(x[0], x[2])
    c, d = plus(x[1], x[3]), turned(minus(x[1], x[3]), sign)
    return [plus(a, c), plus(b, d), minus(a, c), minus(b, d)]


def eight(x, sign):
    even, odd = four(x[0::2], sign), four(x[1::2], sign)
    o1, o3 = odd[1], odd[3]
    odd1 = ((o1[0] - sign * o1[1]) * half_root, (o1[1] + sign * o1[0]) * half_root)
    odd3 = ((-o3[0] - sign * o3[1]) * half_root, (sign * o3[0] - o3[1]) * half_root)
    odd = [odd[0], odd1, turned(odd[2], sign), odd3]
    return [plus(e, o) for e, o in zip(even, odd)] + [minus(e, o) for e, o in zip(even, odd)]


def split(x):
    high = x.astype(bf16)
    return high, (x - high.astype(f32)).astype(bf16)


def product(a, b, dims):
    dot = functools.partial(lax.dot_general, dimension_numbers=(dims, ((), ())), preferred_element_type=f32)
    return dot(a[0], b[0]) + (dot(a[1], b[0]) + dot(a[0], b[1]))


def from_peers(x_ref, pair, matrix, re_ref, im_ref, tiles):
    x = jnp.concatenate([x_ref[pl.ds(2 * pair + part, PEERS, stride=tiles), :] for part in range(2)], axis=0)
    y = product(split(x), matrix, ((0,), (0,)))
    re_ref[...] = y[:, :PEERS]
    im_ref[...] = y[:, PEERS:]


def to_peers(o_ref, pair, matrix, re_ref, im_ref, tiles):
    t = split(jnp.concatenate([re_ref[...], im_ref[...]], axis=1))
    out = product(matrix, t, ((1,), (1,)))
    for part in range(2):
        o_ref[pl.ds(2 * pair + part, PEERS, stride=tiles), :] = out[part * PEERS : (part + 1) * PEERS]


def twisted(value, twist_ref, index, sign):
    if index == 0:
        return value
    c, s = twist_ref[0, index], twist_ref[1, index]
    if sign < 0:
        return (value[0] * c + value[1] * s, value[1] * c - value[0] * s)
    return (value[0] * c - value[1] * s, value[1] * c + value[0] * s)


def strike_forward(take, twist_ref, matrix, o_ref, re_ref, im_ref):
    for pair in range(3):
        for member in range(2):
            plane = 2 * pair + member
            waves = eight([(take(plane, tile), None) for tile in range(GX)], -1.0)
            for k in range(8):
                re, im = waves[k]
                if im is None:
                    im = jnp.zeros_like(re)
                re, im = twisted((re, im), twist_ref, k, -1)
                rows = pl.ds(member * 64 + k * 8, 8)
                re_ref[rows, :] = re
                im_ref[rows, :] = im
        to_peers(o_ref, pair, matrix, re_ref, im_ref, 6)


def strike_inverse(x_ref, twist_ref, matrix, d_ref, re_ref, im_ref, put):
    lane = lane_index((8, PEERS))
    edges = [jnp.zeros((8, PEERS), f32)] * GX
    for pair in range(3):
        from_peers(x_ref, pair, matrix, re_ref, im_ref, TILES)
        for member in range(2):
            plane = 2 * pair + member
            values = []
            for k in range(8):
                rows = pl.ds(member * 64 + k, 8, stride=8)
                values.append(twisted((re_ref[rows, :], im_ref[rows, :]), twist_ref, k, 1))
            field = eight(values, 1.0)
            for tile in range(GX):
                value = field[tile][0]
                d_ref[tile, pl.ds(plane * 8, 8), :] = value
                moved = pltpu.roll(value, plane, 1) if plane else value
                before = (tile + GX - 1) % GX
                edges[before] = jnp.where(lane == plane, moved, edges[before])
                put(plane, tile, value)
    for tile in range(GX):
        d_ref[tile, pl.ds(56, 8), :] = edges[tile]
    x = split(x_ref[pl.ds(6, PEERS, stride=TILES), :])
    y = product(x, (matrix[0][:PEERS], matrix[1][:PEERS]), ((0,), (0,)))
    re_ref[...] = y[:, :PEERS]
    im_ref[...] = y[:, PEERS:]
    values = []
    for k in range(8):
        low, high = pl.ds(k, 8, stride=8), pl.ds(64 + k, 8, stride=8)
        value = (re_ref[low, :] - im_ref[high, :], im_ref[low, :] + re_ref[high, :])
        values.append(twisted(value, twist_ref, k, 1))
    field = eight(values, 1.0)
    for tile in range(GX):
        d_ref[tile, pl.ds(48, 8), :] = field[tile][0]


def forward_kernel(x_ref, mx_ref, twist_ref, o_ref, re_ref, im_ref):
    matrix = (mx_ref[0], mx_ref[1])
    take = lambda plane, tile: x_ref[tile, pl.ds(plane * 16, 8), :]
    strike_forward(take, twist_ref, matrix, o_ref, re_ref, im_ref)


def dip_kernel(carry, x_ref, my_ref, twist_ref, ahead_ref, impedance_ref, *refs):
    now, o_ref, spectrum_ref = refs[:2], refs[2], refs[3]
    re_ref, im_ref, re2_ref, im2_ref, z_ref, tail_ref, sems = refs[3 + carry :]

    def copies(pair):
        jobs = []
        for plane in (2 * pair, 2 * pair + 1):
            side, part = plane // 3, pl.ds(2 * (plane % 3), 2)
            jobs.append((impedance_ref.at[plane], z_ref.at[plane], sems.at[plane, 0]))
            jobs.append((now[side].at[part], tail_ref.at[plane], sems.at[plane, 1]))
        return [pltpu.make_async_copy(*job) for job in jobs]

    arriving = [copies(pair) for pair in range(3)]
    for group in arriving:
        for copy in group:
            copy.start()
    matrix = (my_ref[0], my_ref[1])
    re2_ref[...] = jnp.zeros((PEERS, PEERS), f32)
    im2_ref[...] = jnp.zeros((PEERS, PEERS), f32)
    c8, s8 = ahead_ref[0], ahead_ref[1]
    for pair in range(3):
        from_peers(x_ref, pair, matrix, re_ref, im_ref, 6)
        for copy in arriving[pair]:
            copy.wait()
        for member in range(2):
            plane = 2 * pair + member
            values = []
            for j in range(8):
                rows = pl.ds(member * 64 + j, 8, stride=8)
                values.append(twisted((re_ref[rows, :], im_ref[rows, :]), twist_ref, j, -1))
            spectrum = eight(values, -1.0)
            response = []
            for tile in range(8):
                lanes = pl.ds(tile * PEERS, PEERS)
                z = z_ref[plane, :, lanes]
                re, im = spectrum[tile]
                response.append((tail_ref[plane, 0, :, lanes] - z * re, tail_ref[plane, 1, :, lanes] - z * im))
                if carry:
                    spectrum_ref[2 * plane, :, lanes] = re
                    spectrum_ref[2 * plane + 1, :, lanes] = im
            lines = eight(response, 1.0)
            for j in range(8):
                re, im = twisted(lines[j], twist_ref, j, 1)
                rows = pl.ds(member * 64 + j * 8, 8)
                re_ref[rows, :] = re
                im_ref[rows, :] = im
                if j == 0:
                    re, im = re * c8 - im * s8, im * c8 + re * s8
                    for half, (a, b) in enumerate(((re, im), (im, -re))):
                        rows = pl.ds(half * 64 + plane * 8, 8)
                        re2_ref[rows, :] = a
                        im2_ref[rows, :] = b
        to_peers(o_ref, pair, matrix, re_ref, im_ref, TILES)
    t = split(jnp.concatenate([re2_ref[...], im2_ref[...]], axis=1))
    o_ref[pl.ds(6, PEERS, stride=TILES), :] = product((matrix[0][:PEERS], matrix[1][:PEERS]), t, ((1,), (1,)))


def carry_kernel(spectrum_ref, memory_ref, *refs):
    for plane in range(6):
        side = plane // 3
        for part in range(2):
            row = 2 * (plane % 3) + part
            value = memory_ref[side, 0] * spectrum_ref[2 * plane + part]
            refs[2 + side][row] = refs[side][row] + value


def turn_kernel(x_ref, early_ref, mx_ref, twist_ref, o_ref, d_ref, re_ref, im_ref, plane_ref):
    matrix = (mx_ref[0], mx_ref[1])

    def put(plane, tile, value):
        gain = early_ref[tile, pl.ds(48 + (plane // 3) * 8, 8), :]
        plane_ref[tile, pl.ds(plane * 8, 8), :] = early_ref[tile, pl.ds(plane * 8, 8), :] + gain * value

    strike_inverse(x_ref, twist_ref, matrix, d_ref, re_ref, im_ref, put)
    take = lambda plane, tile: plane_ref[tile, pl.ds(plane * 8, 8), :]
    strike_forward(take, twist_ref, matrix, o_ref, re_ref, im_ref)


def inverse_kernel(x_ref, mx_ref, twist_ref, d_ref, re_ref, im_ref):
    matrix = (mx_ref[0], mx_ref[1])
    strike_inverse(x_ref, twist_ref, matrix, d_ref, re_ref, im_ref, lambda plane, tile, value: None)


def history_kernel(history_ref, memory_ref, now_ref, next_ref):
    lags = history_ref.shape[2]
    for tile in range(8):
        lanes = pl.ds(tile * PEERS, PEERS)
        for part in range(2):
            now = jnp.zeros((8, PEERS), f32)
            later = jnp.zeros((8, PEERS), f32)
            for lag in range(lags):
                value = history_ref[0, 0, lag, part, :, lanes]
                now = now + memory_ref[0, lag, :, lanes] * value
                if lag + 1 < lags:
                    later = later + memory_ref[0, lag + 1, :, lanes] * value
            now_ref[part, :, lanes] = now
            next_ref[part, :, lanes] = later


def pack_kernel(table_ref, velocity_ref, stress_ref, zones_ref, o_ref, v_ref, x_ref, y_ref, z_ref, zone_ref, sems):
    copies = []
    for side in range(2):
        jobs = (
            (velocity_ref.at[:, 3 * side], v_ref.at[side]),
            (stress_ref.at[:, 0, 3 * side], x_ref.at[side]),
            (stress_ref.at[:, 1, 3 * side], y_ref.at[side]),
            (stress_ref.at[:, 2, 2 * side], z_ref.at[side]),
            (zones_ref.at[3 * side], zone_ref.at[side]),
        )
        for number, (source, target) in enumerate(jobs):
            copies.append(pltpu.make_async_copy(source, target, sems.at[side, number]))
    for copy in copies:
        copy.start()
    for copy in copies:
        copy.wait()
    row = lax.broadcasted_iota(jnp.int32, (64, PEERS), 0)
    lane = lane_index((64, PEERS))
    edge = packed_column([x_ref[plane // 3, plane % 3] for plane in range(6)], PEERS - 1, lane)
    for side in range(2):
        zone = zone_ref[side]
        gain = jnp.zeros(zone.shape, f32)
        for index in range(table_ref.shape[1]):
            gain = jnp.where(zone == index, table_ref[1, index], gain)
        gain = gain * time_step
        for c in range(3):
            plane = 3 * side + c
            v, x, y, z = v_ref[side, c], x_ref[side, c], y_ref[side, c], z_ref[side, c]
            behind_x = jnp.where(lane == 0, 0.0, pltpu.roll(x, 1, 1))
            behind_y = jnp.where(row == 0, 0.0, pltpu.roll(y, 1, 0))
            force = (x - behind_x) + (y - behind_y) + (z if side == 0 else -z)
            early = v + gain * force
            for tile in range(GX):
                lines = slice(tile * 8, tile * 8 + 8)
                o_ref[tile, pl.ds(plane * 16, 8), :] = v[lines]
                o_ref[tile, pl.ds(plane * 16 + 8, 8), :] = early[lines]
                o_ref[tile, pl.ds(120 + plane, 1), :] = y_ref[side, c, pl.ds(63, 1), :]
        for tile in range(GX):
            lines = slice(tile * 8, tile * 8 + 8)
            o_ref[tile, pl.ds(96 + 8 * side, 8), :] = -gain[lines] if side == 0 else gain[lines]
            o_ref[tile, pl.ds(126 + side, 1), :] = jnp.zeros((1, PEERS), f32)
            if side == 0:
                o_ref[tile, pl.ds(112, 8), :] = edge[lines]


def lane_index(shape):
    return lax.broadcasted_iota(jnp.int32, shape, len(shape) - 1)


def packed_column(values, column, lane):
    out = jnp.zeros(values[0].shape, f32)
    for k, value in enumerate(values):
        shift = (k - column) % PEERS
        moved = pltpu.roll(value, shift, 1) if shift else value
        out = jnp.where(lane == k, moved, out)
    return out


def zones_kernel(table_ref, zones_ref, x_ref, y_ref, coef_ref, west_ref, south_ref):
    for z in range(4):
        zone = zones_ref[z]
        rows = [jnp.zeros(zone.shape, f32)] * 3
        for index in range(table_ref.shape[1]):
            matched = zone == index
            rows = [jnp.where(matched, table_ref[row, index], rows[row]) for row in range(3)]
        coef_ref[0, z] = rows[0] * time_step
        coef_ref[1, z] = rows[1] * time_step
        coef_ref[2, z] = rows[2]
    lane = lane_index((64, PEERS))
    west_ref[...] = packed_column([x_ref[k // 4, 0, k % 4] for k in range(12)], PEERS - 1, lane)
    for k in range(12):
        south_ref[pl.ds(k, 1), :] = y_ref[k // 4, 0, k % 4, pl.ds(7, 1), :]


def pushed(c, z, lane, row, velocity, stress_ref, west, south_ref, gain):
    k = c * 4 + z
    x, y = stress_ref[c, 0, z], stress_ref[c, 1, z]
    edge = pltpu.roll(west, PEERS - k, 1) if k else west
    behind_x = jnp.where(lane == 0, edge, pltpu.roll(x, 1, 1))
    behind_y = jnp.where(row == 0, south_ref[pl.ds(k, 1), :], pltpu.roll(y, 1, 0))
    force = x - behind_x + y - behind_y
    if z < 3:
        force = force + stress_ref[c, 2, z]
    if z > 0:
        force = force - stress_ref[c, 2, z - 1]
    return velocity + gain * force


def early_kernel(velocity_ref, stress_ref, west_ref, south_ref, coef_ref, early_ref, east_ref, north_ref):
    lane = lane_index((64, PEERS))
    row = lax.broadcasted_iota(jnp.int32, (64, PEERS), 0)
    west = west_ref[...]
    for c in range(3):
        for z in range(4):
            early_ref[c, z] = pushed(
                c, z, lane, row, velocity_ref[c, z], stress_ref, west, south_ref, coef_ref[1, z]
            )
    fields = [early_ref.at[k // 4, k % 4] for k in range(12)] + [coef_ref.at[1, 0], coef_ref.at[1, 3]]
    east_ref[...] = packed_column([field[...] for field in fields], 0, lane)
    for k, field in enumerate(fields):
        north_ref[pl.ds(k, 1), :] = field[pl.ds(0, 1), :]
    north_ref[pl.ds(14, 2), :] = jnp.zeros((2, PEERS), f32)


def feed_kernel(rows_ref, south_ref, feed_ref):
    lane = lane_index((8, PEERS))
    row = lax.broadcasted_iota(jnp.int32, (8, PEERS), 0)
    for tile in range(GX):
        edge = rows_ref[(tile + GX - 1) % GX, pl.ds(112, 8), :]
        for side in range(2):
            signed = rows_ref[tile, pl.ds(96 + 8 * side, 8), :]
            feed_ref[tile, pl.ds(48 + 8 * side, 8), :] = signed
            gain = -signed if side == 0 else signed
            for c in range(3):
                plane = 3 * side + c
                west = pltpu.roll(edge, PEERS - plane, 1) if plane else edge
                behind = jnp.where(lane == 0, west, 0.0)
                south = jnp.where(row == 0, south_ref[tile, pl.ds(plane, 1), :], 0.0)
                early = rows_ref[tile, pl.ds(plane * 16 + 8, 8), :]
                feed_ref[tile, pl.ds(plane * 8, 8), :] = early - gain * (behind + south)


def cells_kernel(rims, early_ref, east_ref, north_ref, d_ref, coef_ref, stress_ref, mask_ref, v_ref, o_ref, *refs):
    lane = lane_index((64, PEERS))
    row = lax.broadcasted_iota(jnp.int32, (64, PEERS), 0)
    for c in range(3):
        for z in range(4):
            v_ref[c, z] = early_ref[c, z]
    for tile in range(GX):
        rows = pl.ds(tile * 8, 8)
        for plane in range(6):
            c, z = plane % 3, 3 * (plane // 3)
            push = coef_ref[1, z, rows, :] * d_ref[tile, pl.ds(plane * 8, 8), :]
            base = early_ref[c, z, rows, :]
            v_ref[c, z, rows, :] = base - push if z == 0 else base + push
    east = east_ref[...]
    edge = jnp.concatenate([d_ref[tile, pl.ds(56, 8), :] for tile in range(GX)], axis=0)
    last = lambda value, k: pltpu.roll(value, PEERS - 1 - k, 1)
    for z in range(4):
        rigidity = coef_ref[0, z]
        cohesion = coef_ref[2, z]
        keep = [mask_ref[d, z].astype(f32) for d in range(3)]
        total = jnp.zeros((64, PEERS), f32)
        trial = []
        for c in range(3):
            k = c * 4 + z
            v = v_ref[c, z]
            past_x, past_y = last(east, k), north_ref[pl.ds(k, 1), :]
            if z in (0, 3):
                plane, gain = c + z, 12 if z == 0 else 13
                push_x = last(east, gain) * last(edge, plane)
                push_y = north_ref[pl.ds(gain, 1), :] * d_ref[GX - 1, pl.ds(48 + plane, 1), :]
                past_x = past_x - push_x if z == 0 else past_x + push_x
                past_y = past_y - push_y if z == 0 else past_y + push_y
            ahead_x = jnp.where(lane == PEERS - 1, past_x, pltpu.roll(v, PEERS - 1, 1))
            ahead_y = jnp.where(row == 63, past_y, pltpu.roll(v, 63, 0))
            tx = keep[0] * (stress_ref[c, 0, z] + rigidity * (ahead_x - v))
            ty = keep[1] * (stress_ref[c, 1, z] + rigidity * (ahead_y - v))
            if z < 3:
                tz = keep[2] * (stress_ref[c, 2, z] + rigidity * (v_ref[c, z + 1] - v))
            else:
                pulled = [d_ref[tile, pl.ds((3 + c) * 8, 8), :] for tile in range(GX)]
                tz = keep[2] * jnp.concatenate(pulled, axis=0)
            trial.append((tx, ty, tz))
            total = total + (tx * tx + ty * ty + tz * tz)
        factor = cohesion / jnp.maximum(jnp.sqrt(total), cohesion)
        for c in range(3):
            for d in range(3):
                o_ref[c, d, z] = trial[c][d] * factor
    if rims:
        west_ref, south_ref = refs
        west_ref[...] = packed_column([o_ref[k // 4, 0, k % 4] for k in range(12)], PEERS - 1, lane)
        for k in range(12):
            south_ref[pl.ds(k, 1), :] = o_ref[k // 4, 1, k % 4, pl.ds(63, 1), :]
        south_ref[pl.ds(12, 4), :] = jnp.zeros((4, PEERS), f32)


def shape(*dims):
    return jax.ShapeDtypeStruct(dims, f32)


WORK = [pltpu.VMEM((PEERS, PEERS), f32), pltpu.VMEM((PEERS, PEERS), f32)]


def near(*dims):
    return pltpu.VMEM(dims, f32)


def room(size):
    return pltpu.CompilerParams(vmem_limit_bytes=size << 20)


def far(*dims):
    return pltpu.HBM(dims, f32)


def held(arrays, space):
    return [pltpu.with_memory_space_constraint(a, space) for a in arrays]


def call(kernel, outs, *args, scratch=(), close=True):
    if close:
        args = held(args, pltpu.VMEM)
    return pl.pallas_call(kernel, out_shape=outs, scratch_shapes=list(scratch), compiler_params=room(8))(*args)


def exchange_all(value):
    tiles = value.shape[0] // PEERS
    blocks = value.reshape(PEERS, 1, tiles * PEERS)
    blocks = lax.all_to_all(blocks, both, split_axis=0, concat_axis=0, tiled=True)
    return blocks.reshape(tiles * PEERS, PEERS)


def exchange_row(value):
    return lax.all_to_all(value, "gx", split_axis=0, concat_axis=0, tiled=True)


def shifted(value, axis, steps):
    count = lax.axis_size(axis)
    return lax.ppermute(value, axis, [(source, (source + steps) % count) for source in range(count)])


def pack(zone_table, velocity, stress, zones):
    whole = pl.BlockSpec(memory_space=pltpu.HBM)
    field = pltpu.VMEM((2, 3, 64, PEERS), f32)
    return pl.pallas_call(
        pack_kernel,
        in_specs=[pl.BlockSpec(memory_space=pltpu.SMEM), whole, whole, whole],
        out_shape=near(GX, PEERS, PEERS),
        scratch_shapes=[field] * 4 + [pltpu.VMEM((2, 64, PEERS), jnp.int32), pltpu.SemaphoreType.DMA((2, 5))],
        compiler_params=room(16),
        name="pack",
    )(*held((zone_table, velocity, stress, zones), pltpu.HBM))


def zones_of(zone_table, zones, stress):
    whole = lambda *dims: pl.BlockSpec(dims, lambda i: (0,) * len(dims))
    return pl.pallas_call(
        zones_kernel,
        grid=(1,),
        in_specs=[
            pl.BlockSpec(memory_space=pltpu.SMEM),
            whole(4, 64, PEERS),
            pl.BlockSpec((3, 1, 4, 64, PEERS), lambda i: (0, 0, 0, 0, 0)),
            pl.BlockSpec((3, 1, 4, 8, PEERS), lambda i: (0, 1, 0, 7, 0)),
        ],
        out_specs=[whole(3, 4, 64, PEERS), whole(64, PEERS), whole(16, PEERS)],
        out_shape=[far(3, 4, 64, PEERS), far(64, PEERS), far(16, PEERS)],
        compiler_params=room(16),
        name="zones",
    )(*held((zone_table, zones, stress, stress), pltpu.HBM))


def tails_of(history, memory, plane):
    out_spec = pl.BlockSpec((2, 8, 1024), lambda c: (c, 0, 0))
    return pl.pallas_call(
        history_kernel,
        grid=(3,),
        in_specs=[
            pl.BlockSpec((1, 1, 31, 2, 8, 1024), lambda c: (plane, c, 0, 0, 0, 0)),
            pl.BlockSpec((1, 31, 8, 1024), lambda c: (plane, 0, 0, 0)),
        ],
        out_specs=[out_spec, out_spec],
        out_shape=[far(6, 8, 1024)] * 2,
        compiler_params=room(16),
    )(*held((history, memory), pltpu.HBM))


def steps(velocity, stress, face_mask, zones, zone_table, impedance, memory, history):
    mx, my, twist, ahead = tables()
    impedance = impedance.reshape(6, 8, 1024)
    sending, returning = near(6 * PEERS, PEERS), near(TILES * PEERS, PEERS)
    dma = pltpu.SemaphoreType.DMA
    square = pltpu.VMEM((PEERS, PEERS), f32)

    def make_dip(carry, sent, *operands):
        spec = lambda space, count: [pl.BlockSpec(memory_space=space)] * count
        pairs = pltpu.VMEM((6, 2, 8, 1024), f32)
        outs = [returning] + [near(12, 8, 1024)] * carry
        return pl.pallas_call(
            functools.partial(dip_kernel, carry),
            in_specs=spec(pltpu.VMEM, 4) + spec(pltpu.HBM, len(operands)),
            out_specs=spec(pltpu.VMEM, len(outs)),
            out_shape=outs,
            scratch_shapes=[square] * 4 + [pltpu.VMEM((6, 8, 1024), f32), pairs, dma((6, 2))],
            compiler_params=room(8),
        )(*held((sent, my, twist, ahead), pltpu.VMEM), *held(operands, pltpu.HBM))

    def make_carry(spectrum, memory, later):
        whole = lambda *dims: pl.BlockSpec(dims, lambda i: (0,) * len(dims))
        wave = whole(6, 8, 1024)
        return pl.pallas_call(
            carry_kernel,
            grid=(1,),
            in_specs=[whole(12, 8, 1024), whole(2, 1, 8, 1024), wave, wave],
            out_specs=[wave, wave],
            out_shape=[far(6, 8, 1024)] * 2,
            compiler_params=room(8),
            name="carry",
        )(spectrum, *held((memory, *later), pltpu.HBM))

    def make_early(velocity, stress, west, south, name):
        outs = [(far if name == "early0" else near)(3, 4, 64, PEERS), far(64, PEERS), far(16, PEERS)]
        velocity, stress, coef_far = held((velocity, stress, coef), pltpu.HBM)
        return call(early_kernel, outs, velocity, stress, west, south, coef_far, close=False)

    def make_cells(rims, early, east, north, traction, *fields):
        outs = [shape(3, 4, 64, PEERS), shape(3, 3, 4, 64, PEERS)]
        if rims:
            outs = [far(3, 4, 64, PEERS), far(3, 3, 4, 64, PEERS), far(64, PEERS), far(16, PEERS)]
            early, *fields = held((early, *fields), pltpu.VMEM)
        operands = (early, east, north, traction, *fields)
        return call(functools.partial(cells_kernel, rims), outs, *operands, close=not rims)

    rows = exchange_row(pack(zone_table, velocity, stress, zones))
    coef, west, south = zones_of(zone_table, zones, stress)
    west, south = shifted(west, "gx", 1), shifted(south, "gy", 1)
    now, later = zip(tails_of(history, memory, 0), tails_of(history, memory, 1))
    sent = exchange_all(call(forward_kernel, sending, rows, mx, twist, scratch=WORK))
    onward = [((GX - 1) * GY + h, (h + 1) % GY) for h in range(GY)]
    above = lax.ppermute(rows[:, 120:], both, onward)
    early, east, north = make_early(velocity, stress, west, south, "early0")
    east, north = shifted(east, "gx", -1), shifted(north, "gy", -1)
    lines, spectrum = make_dip(True, sent, impedance, *now)
    later = make_carry(spectrum, memory, later)
    lines = exchange_all(lines)
    feed = call(feed_kernel, near(GX, 64, PEERS), rows, above)
    sending1, traction = call(
        turn_kernel,
        [sending, near(GX, 64, PEERS)],
        lines, feed, mx, twist,
        scratch=[square] * 2 + [pltpu.VMEM((GX, 48, PEERS), f32)],
    )
    sent = exchange_all(sending1)
    traction = exchange_row(traction)
    (lines,) = make_dip(False, sent, impedance, *later)
    lines = exchange_all(lines)
    velocity, stress, west, south = make_cells(True, early, east, north, traction, coef, stress, face_mask)
    west, south = shifted(west, "gx", 1), shifted(south, "gy", 1)
    early, east, north = make_early(velocity, stress, west, south, "early1")
    east, north = shifted(east, "gx", -1), shifted(north, "gy", -1)
    traction = call(inverse_kernel, near(GX, 64, PEERS), lines, mx, twist, scratch=[square] * 2)
    traction = exchange_row(traction)
    velocity, stress = make_cells(False, early, east, north, traction, coef, stress, face_mask)
    return (velocity, stress)


def solution(mesh):
    in_specs = (
        P(None, None, "gy", "gx"),
        P(None, None, None, "gy", "gx"),
        P(None, None, "gy", "gx"),
        P(None, "gy", "gx"),
        P(),
        P(None, None, both, None),
        P(None, None, both, None),
        P(None, None, None, None, both, None),
    )
    out_specs = (P(None, None, "gy", "gx"), P(None, None, None, "gy", "gx"))
    return jax.shard_map(steps, mesh=mesh, in_specs=in_specs, out_specs=out_specs, check_vma=False)
```

```python
import functools
import math

import jax
import jax.numpy as jnp
import numpy as np
from jax import lax
from jax.experimental import pallas as pl
from jax.experimental.pallas import tpu as pltpu
from jax.sharding import PartitionSpec as P


time_step = 0.2
GX = 8
GY = 16
PEERS = 128
f32 = jnp.float32
bf16 = jnp.bfloat16
TILES = 7
both = ("gx", "gy")
half_root = math.sqrt(0.5)


def halves(table):
    high = jnp.asarray(table, f32).astype(bf16)
    low = (jnp.asarray(table, f32) - high.astype(f32)).astype(bf16)
    return jnp.stack([high, low])


def tables():
    index = np.arange(PEERS)
    angle = 2.0 * np.pi * (np.outer(index, index) % PEERS) / PEERS
    c, s = np.cos(angle) / 32.0, np.sin(angle) / 32.0
    along_x = np.block([[c, s], [-s, c]])
    place = 8 * (index % GY) + index // GY
    angle = 2.0 * np.pi * (np.outer(place, index) % PEERS) / PEERS
    c, s = np.cos(angle) / 32.0, np.sin(angle) / 32.0
    along_y = np.block([[c, -s], [s, c]])
    turn = 2.0 * np.pi * np.outer(np.arange(8), index) / 1024.0
    twist = np.stack([np.cos(turn), np.sin(turn)])
    twist = np.broadcast_to(twist[:, :, None, :], (2, 8, 8, PEERS))
    turn = 2.0 * np.pi * index / PEERS
    ahead = np.broadcast_to(np.stack([np.cos(turn), np.sin(turn)])[:, None, :], (2, 8, PEERS))
    return halves(along_x), halves(along_y), jnp.asarray(twist, f32), jnp.asarray(ahead, f32)


def plus(a, b):
    imag = a[1] if b[1] is None else b[1] if a[1] is None else a[1] + b[1]
    return (a[0] + b[0], imag)


def minus(a, b):
    imag = a[1] if b[1] is None else -b[1] if a[1] is None else a[1] - b[1]
    return (a[0] - b[0], imag)


def turned(a, sign):
    if a[1] is None:
        return (jnp.zeros_like(a[0]), a[0] if sign > 0 else -a[0])
    return (-a[1], a[0]) if sign > 0 else (a[1], -a[0])


def four(x, sign):
    a, b = plus(x[0], x[2]), minus(x[0], x[2])
    c, d = plus(x[1], x[3]), turned(minus(x[1], x[3]), sign)
    return [plus(a, c), plus(b, d), minus(a, c), minus(b, d)]


def eight(x, sign):
    even, odd = four(x[0::2], sign), four(x[1::2], sign)
    o1, o3 = odd[1], odd[3]
    odd1 = ((o1[0] - sign * o1[1]) * half_root, (o1[1] + sign * o1[0]) * half_root)
    odd3 = ((-o3[0] - sign * o3[1]) * half_root, (sign * o3[0] - o3[1]) * half_root)
    odd = [odd[0], odd1, turned(odd[2], sign), odd3]
    return [plus(e, o) for e, o in zip(even, odd)] + [minus(e, o) for e, o in zip(even, odd)]


def split(x):
    high = x.astype(bf16)
    return high, (x - high.astype(f32)).astype(bf16)


def product(a, b, dims):
    dot = functools.partial(lax.dot_general, dimension_numbers=(dims, ((), ())), preferred_element_type=f32)
    return dot(a[0], b[0]) + (dot(a[1], b[0]) + dot(a[0], b[1]))


def from_peers(x_ref, pair, matrix, re_ref, im_ref, tiles):
    x = jnp.concatenate([x_ref[pl.ds(2 * pair + part, PEERS, stride=tiles), :] for part in range(2)], axis=0)
    y = product(split(x), matrix, ((0,), (0,)))
    re_ref[...] = y[:, :PEERS]
    im_ref[...] = y[:, PEERS:]


def to_peers(o_ref, pair, matrix, re_ref, im_ref, tiles):
    t = split(jnp.concatenate([re_ref[...], im_ref[...]], axis=1))
    out = product(matrix, t, ((1,), (1,)))
    for part in range(2):
        o_ref[pl.ds(2 * pair + part, PEERS, stride=tiles), :] = out[part * PEERS : (part + 1) * PEERS]


def twisted(value, twist_ref, index, sign):
    if index == 0:
        return value
    c, s = twist_ref[0, index], twist_ref[1, index]
    if sign < 0:
        return (value[0] * c + value[1] * s, value[1] * c - value[0] * s)
    return (value[0] * c - value[1] * s, value[1] * c + value[0] * s)


def strike_forward(take, twist_ref, matrix, o_ref, re_ref, im_ref):
    for pair in range(3):
        for member in range(2):
            plane = 2 * pair + member
            waves = eight([(take(plane, tile), None) for tile in range(GX)], -1.0)
            for k in range(8):
                re, im = waves[k]
                if im is None:
                    im = jnp.zeros_like(re)
                re, im = twisted((re, im), twist_ref, k, -1)
                rows = pl.ds(member * 64 + k * 8, 8)
                re_ref[rows, :] = re
                im_ref[rows, :] = im
        to_peers(o_ref, pair, matrix, re_ref, im_ref, TILES)


def strike_inverse(x_ref, twist_ref, matrix, d_ref, re_ref, im_ref, put):
    lane = lane_index((8, PEERS))
    edges = [jnp.zeros((8, PEERS), f32)] * GX
    for pair in range(3):
        from_peers(x_ref, pair, matrix, re_ref, im_ref, TILES)
        for member in range(2):
            plane = 2 * pair + member
            values = []
            for k in range(8):
                rows = pl.ds(member * 64 + k, 8, stride=8)
                values.append(twisted((re_ref[rows, :], im_ref[rows, :]), twist_ref, k, 1))
            field = eight(values, 1.0)
            for tile in range(GX):
                value = field[tile][0]
                d_ref[tile, pl.ds(plane * 8, 8), :] = value
                moved = pltpu.roll(value, plane, 1) if plane else value
                before = (tile + GX - 1) % GX
                edges[before] = jnp.where(lane == plane, moved, edges[before])
                put(plane, tile, value)
    for tile in range(GX):
        d_ref[tile, pl.ds(56, 8), :] = edges[tile]
    x = split(x_ref[pl.ds(6, PEERS, stride=TILES), :])
    y = product(x, (matrix[0][:PEERS], matrix[1][:PEERS]), ((0,), (0,)))
    re_ref[...] = y[:, :PEERS]
    im_ref[...] = y[:, PEERS:]
    values = []
    for k in range(8):
        low, high = pl.ds(k, 8, stride=8), pl.ds(64 + k, 8, stride=8)
        value = (re_ref[low, :] - im_ref[high, :], im_ref[low, :] + re_ref[high, :])
        values.append(twisted(value, twist_ref, k, 1))
    field = eight(values, 1.0)
    for tile in range(GX):
        d_ref[tile, pl.ds(48, 8), :] = field[tile][0]


def forward_kernel(x_ref, mx_ref, twist_ref, o_ref, re_ref, im_ref):
    matrix = (mx_ref[0], mx_ref[1])
    take = lambda plane, tile: x_ref[tile, pl.ds(plane * 16, 8), :]
    strike_forward(take, twist_ref, matrix, o_ref, re_ref, im_ref)


def dip_kernel(carry, x_ref, my_ref, twist_ref, ahead_ref, impedance_ref, *refs):
    now, o_ref, spectrum_ref = refs[:2], refs[2], refs[3]
    re_ref, im_ref, re2_ref, im2_ref, z_ref, tail_ref, sems = refs[3 + carry :]

    def copies(pair):
        jobs = []
        for plane in (2 * pair, 2 * pair + 1):
            side, part = plane // 3, pl.ds(2 * (plane % 3), 2)
            jobs.append((impedance_ref.at[plane], z_ref.at[plane], sems.at[plane, 0]))
            jobs.append((now[side].at[part], tail_ref.at[plane], sems.at[plane, 1]))
        return [pltpu.make_async_copy(*job) for job in jobs]

    arriving = [copies(pair) for pair in range(3)]
    for group in arriving:
        for copy in group:
            copy.start()
    matrix = (my_ref[0], my_ref[1])
    re2_ref[...] = jnp.zeros((PEERS, PEERS), f32)
    im2_ref[...] = jnp.zeros((PEERS, PEERS), f32)
    c8, s8 = ahead_ref[0], ahead_ref[1]
    for pair in range(3):
        from_peers(x_ref, pair, matrix, re_ref, im_ref, TILES)
        for copy in arriving[pair]:
            copy.wait()
        for member in range(2):
            plane = 2 * pair + member
            values = []
            for j in range(8):
                rows = pl.ds(member * 64 + j, 8, stride=8)
                values.append(twisted((re_ref[rows, :], im_ref[rows, :]), twist_ref, j, -1))
            spectrum = eight(values, -1.0)
            response = []
            for tile in range(8):
                lanes = pl.ds(tile * PEERS, PEERS)
                z = z_ref[plane, :, lanes]
                re, im = spectrum[tile]
                response.append((tail_ref[plane, 0, :, lanes] - z * re, tail_ref[plane, 1, :, lanes] - z * im))
                if carry:
                    spectrum_ref[2 * plane, :, lanes] = re
                    spectrum_ref[2 * plane + 1, :, lanes] = im
            lines = eight(response, 1.0)
            for j in range(8):
                re, im = twisted(lines[j], twist_ref, j, 1)
                rows = pl.ds(member * 64 + j * 8, 8)
                re_ref[rows, :] = re
                im_ref[rows, :] = im
                if j == 0:
                    re, im = re * c8 - im * s8, im * c8 + re * s8
                    for half, (a, b) in enumerate(((re, im), (im, -re))):
                        rows = pl.ds(half * 64 + plane * 8, 8)
                        re2_ref[rows, :] = a
                        im2_ref[rows, :] = b
        to_peers(o_ref, pair, matrix, re_ref, im_ref, TILES)
    t = split(jnp.concatenate([re2_ref[...], im2_ref[...]], axis=1))
    o_ref[pl.ds(6, PEERS, stride=TILES), :] = product((matrix[0][:PEERS], matrix[1][:PEERS]), t, ((1,), (1,)))


def carry_kernel(spectrum_ref, memory_ref, *refs):
    for plane in range(6):
        side = plane // 3
        for part in range(2):
            row = 2 * (plane % 3) + part
            value = memory_ref[side, 0] * spectrum_ref[2 * plane + part]
            refs[2 + side][row] = refs[side][row] + value


def turn_kernel(x_ref, early_ref, mx_ref, twist_ref, o_ref, d_ref, re_ref, im_ref, plane_ref):
    matrix = (mx_ref[0], mx_ref[1])

    def put(plane, tile, value):
        gain = early_ref[tile, pl.ds(48 + (plane // 3) * 8, 8), :]
        plane_ref[tile, pl.ds(plane * 8, 8), :] = early_ref[tile, pl.ds(plane * 8, 8), :] + gain * value

    strike_inverse(x_ref, twist_ref, matrix, d_ref, re_ref, im_ref, put)
    take = lambda plane, tile: plane_ref[tile, pl.ds(plane * 8, 8), :]
    strike_forward(take, twist_ref, matrix, o_ref, re_ref, im_ref)


def inverse_kernel(x_ref, mx_ref, twist_ref, d_ref, re_ref, im_ref):
    matrix = (mx_ref[0], mx_ref[1])
    strike_inverse(x_ref, twist_ref, matrix, d_ref, re_ref, im_ref, lambda plane, tile, value: None)


def history_kernel(side, history_ref, memory_ref, now_ref, next_ref, h_ref, m_ref, sems):
    lags = h_ref.shape[1]
    chunks = [(0, 11), (11, 11), (22, 9)]
    copies = [pltpu.make_async_copy(memory_ref.at[side], m_ref, sems.at[9])]
    for c in range(3):
        for number, (begin, count) in enumerate(chunks):
            span = pl.ds(begin, count)
            copies.append(
                pltpu.make_async_copy(history_ref.at[side, c, span], h_ref.at[c, span], sems.at[3 * c + number])
            )
    for copy in copies:
        copy.start()
    copies[0].wait()
    for c in range(3):
        for number, (begin, count) in enumerate(chunks):
            copies[1 + 3 * c + number].wait()
            for tile in range(8):
                lanes = pl.ds(tile * PEERS, PEERS)
                for part in range(2):
                    row = 2 * c + part
                    now = now_ref[row, :, lanes] if begin else jnp.zeros((8, PEERS), f32)
                    later = next_ref[row, :, lanes] if begin else jnp.zeros((8, PEERS), f32)
                    for lag in range(begin, begin + count):
                        value = h_ref[c, lag, part, :, lanes]
                        now = now + m_ref[lag, :, lanes] * value
                        if lag + 1 < lags:
                            later = later + m_ref[lag + 1, :, lanes] * value
                    now_ref[row, :, lanes] = now
                    next_ref[row, :, lanes] = later


def pack_kernel(table_ref, velocity_ref, stress_ref, zones_ref, o_ref, v_ref, x_ref, y_ref, z_ref, zone_ref, sems):
    copies = []
    for side in range(2):
        jobs = (
            (velocity_ref.at[:, 3 * side], v_ref.at[side]),
            (stress_ref.at[:, 0, 3 * side], x_ref.at[side]),
            (stress_ref.at[:, 1, 3 * side], y_ref.at[side]),
            (stress_ref.at[:, 2, 2 * side], z_ref.at[side]),
            (zones_ref.at[3 * side], zone_ref.at[side]),
        )
        for number, (source, target) in enumerate(jobs):
            copies.append(pltpu.make_async_copy(source, target, sems.at[side, number]))
    for copy in copies:
        copy.start()
    for copy in copies:
        copy.wait()
    row = lax.broadcasted_iota(jnp.int32, (64, PEERS), 0)
    lane = lane_index((64, PEERS))
    edge = packed_column([x_ref[plane // 3, plane % 3] for plane in range(6)], PEERS - 1, lane)
    for side in range(2):
        zone = zone_ref[side]
        gain = jnp.zeros(zone.shape, f32)
        for index in range(table_ref.shape[1]):
            gain = jnp.where(zone == index, table_ref[1, index], gain)
        gain = gain * time_step
        for c in range(3):
            plane = 3 * side + c
            v, x, y, z = v_ref[side, c], x_ref[side, c], y_ref[side, c], z_ref[side, c]
            behind_x = jnp.where(lane == 0, 0.0, pltpu.roll(x, 1, 1))
            behind_y = jnp.where(row == 0, 0.0, pltpu.roll(y, 1, 0))
            force = (x - behind_x) + (y - behind_y) + (z if side == 0 else -z)
            early = v + gain * force
            for tile in range(GX):
                lines = slice(tile * 8, tile * 8 + 8)
                o_ref[tile, pl.ds(plane * 16, 8), :] = v[lines]
                o_ref[tile, pl.ds(plane * 16 + 8, 8), :] = early[lines]
                o_ref[tile, pl.ds(120 + plane, 1), :] = y_ref[side, c, pl.ds(63, 1), :]
        for tile in range(GX):
            lines = slice(tile * 8, tile * 8 + 8)
            o_ref[tile, pl.ds(96 + 8 * side, 8), :] = -gain[lines] if side == 0 else gain[lines]
            o_ref[tile, pl.ds(126 + side, 1), :] = jnp.zeros((1, PEERS), f32)
            if side == 0:
                o_ref[tile, pl.ds(112, 8), :] = edge[lines]


def lane_index(shape):
    return lax.broadcasted_iota(jnp.int32, shape, len(shape) - 1)


def packed_column(values, column, lane):
    out = jnp.zeros(values[0].shape, f32)
    for k, value in enumerate(values):
        shift = (k - column) % PEERS
        moved = pltpu.roll(value, shift, 1) if shift else value
        out = jnp.where(lane == k, moved, out)
    return out


def zones_kernel(table_ref, zones_ref, x_ref, y_ref, coef_ref, west_ref, south_ref):
    for z in range(4):
        zone = zones_ref[z]
        rows = [jnp.zeros(zone.shape, f32)] * 3
        for index in range(table_ref.shape[1]):
            matched = zone == index
            rows = [jnp.where(matched, table_ref[row, index], rows[row]) for row in range(3)]
        coef_ref[0, z] = rows[0] * time_step
        coef_ref[1, z] = rows[1] * time_step
        coef_ref[2, z] = rows[2]
    lane = lane_index((64, PEERS))
    west_ref[...] = packed_column([x_ref[k // 4, 0, k % 4] for k in range(12)], PEERS - 1, lane)
    for k in range(12):
        south_ref[pl.ds(k, 1), :] = y_ref[k // 4, 0, k % 4, pl.ds(7, 1), :]


def pushed(c, z, lane, row, velocity, stress_ref, west, south_ref, gain):
    k = c * 4 + z
    x, y = stress_ref[c, 0, z], stress_ref[c, 1, z]
    edge = pltpu.roll(west, PEERS - k, 1) if k else west
    behind_x = jnp.where(lane == 0, edge, pltpu.roll(x, 1, 1))
    behind_y = jnp.where(row == 0, south_ref[pl.ds(k, 1), :], pltpu.roll(y, 1, 0))
    force = x - behind_x + y - behind_y
    if z < 3:
        force = force + stress_ref[c, 2, z]
    if z > 0:
        force = force - stress_ref[c, 2, z - 1]
    return velocity + gain * force


def early_kernel(velocity_ref, stress_ref, west_ref, south_ref, coef_ref, early_ref, east_ref, north_ref):
    lane = lane_index((64, PEERS))
    row = lax.broadcasted_iota(jnp.int32, (64, PEERS), 0)
    west = west_ref[...]
    for c in range(3):
        for z in range(4):
            early_ref[c, z] = pushed(
                c, z, lane, row, velocity_ref[c, z], stress_ref, west, south_ref, coef_ref[1, z]
            )
    fields = [early_ref.at[k // 4, k % 4] for k in range(12)] + [coef_ref.at[1, 0], coef_ref.at[1, 3]]
    east_ref[...] = packed_column([field[...] for field in fields], 0, lane)
    for k, field in enumerate(fields):
        north_ref[pl.ds(k, 1), :] = field[pl.ds(0, 1), :]
    north_ref[pl.ds(14, 2), :] = jnp.zeros((2, PEERS), f32)


def feed_kernel(rows_ref, south_ref, feed_ref):
    lane = lane_index((8, PEERS))
    row = lax.broadcasted_iota(jnp.int32, (8, PEERS), 0)
    for tile in range(GX):
        edge = rows_ref[(tile + GX - 1) % GX, pl.ds(112, 8), :]
        for side in range(2):
            signed = rows_ref[tile, pl.ds(96 + 8 * side, 8), :]
            feed_ref[tile, pl.ds(48 + 8 * side, 8), :] = signed
            gain = -signed if side == 0 else signed
            for c in range(3):
                plane = 3 * side + c
                west = pltpu.roll(edge, PEERS - plane, 1) if plane else edge
                behind = jnp.where(lane == 0, west, 0.0)
                south = jnp.where(row == 0, south_ref[tile, pl.ds(plane, 1), :], 0.0)
                early = rows_ref[tile, pl.ds(plane * 16 + 8, 8), :]
                feed_ref[tile, pl.ds(plane * 8, 8), :] = early - gain * (behind + south)


def cells_kernel(rims, early_ref, east_ref, north_ref, d_ref, coef_ref, stress_ref, mask_ref, v_ref, o_ref, *refs):
    lane = lane_index((64, PEERS))
    row = lax.broadcasted_iota(jnp.int32, (64, PEERS), 0)
    for c in range(3):
        for z in range(4):
            v_ref[c, z] = early_ref[c, z]
    for tile in range(GX):
        rows = pl.ds(tile * 8, 8)
        for plane in range(6):
            c, z = plane % 3, 3 * (plane // 3)
            push = coef_ref[1, z, rows, :] * d_ref[tile, pl.ds(plane * 8, 8), :]
            base = early_ref[c, z, rows, :]
            v_ref[c, z, rows, :] = base - push if z == 0 else base + push
    east = east_ref[...]
    edge = jnp.concatenate([d_ref[tile, pl.ds(56, 8), :] for tile in range(GX)], axis=0)
    last = lambda value, k: pltpu.roll(value, PEERS - 1 - k, 1)
    for z in range(4):
        rigidity = coef_ref[0, z]
        cohesion = coef_ref[2, z]
        keep = [mask_ref[d, z].astype(f32) for d in range(3)]
        total = jnp.zeros((64, PEERS), f32)
        trial = []
        for c in range(3):
            k = c * 4 + z
            v = v_ref[c, z]
            past_x, past_y = last(east, k), north_ref[pl.ds(k, 1), :]
            if z in (0, 3):
                plane, gain = c + z, 12 if z == 0 else 13
                push_x = last(east, gain) * last(edge, plane)
                push_y = north_ref[pl.ds(gain, 1), :] * d_ref[GX - 1, pl.ds(48 + plane, 1), :]
                past_x = past_x - push_x if z == 0 else past_x + push_x
                past_y = past_y - push_y if z == 0 else past_y + push_y
            ahead_x = jnp.where(lane == PEERS - 1, past_x, pltpu.roll(v, PEERS - 1, 1))
            ahead_y = jnp.where(row == 63, past_y, pltpu.roll(v, 63, 0))
            tx = keep[0] * (stress_ref[c, 0, z] + rigidity * (ahead_x - v))
            ty = keep[1] * (stress_ref[c, 1, z] + rigidity * (ahead_y - v))
            if z < 3:
                tz = keep[2] * (stress_ref[c, 2, z] + rigidity * (v_ref[c, z + 1] - v))
            else:
                pulled = [d_ref[tile, pl.ds((3 + c) * 8, 8), :] for tile in range(GX)]
                tz = keep[2] * jnp.concatenate(pulled, axis=0)
            trial.append((tx, ty, tz))
            total = total + (tx * tx + ty * ty + tz * tz)
        factor = cohesion / jnp.maximum(jnp.sqrt(total), cohesion)
        for c in range(3):
            for d in range(3):
                o_ref[c, d, z] = trial[c][d] * factor
    if rims:
        west_ref, south_ref = refs
        west_ref[...] = packed_column([o_ref[k // 4, 0, k % 4] for k in range(12)], PEERS - 1, lane)
        for k in range(12):
            south_ref[pl.ds(k, 1), :] = o_ref[k // 4, 1, k % 4, pl.ds(63, 1), :]
        south_ref[pl.ds(12, 4), :] = jnp.zeros((4, PEERS), f32)


def shape(*dims):
    return jax.ShapeDtypeStruct(dims, f32)


WORK = [pltpu.VMEM((PEERS, PEERS), f32), pltpu.VMEM((PEERS, PEERS), f32)]


def near(*dims):
    return pltpu.VMEM(dims, f32)


def room(size):
    return pltpu.CompilerParams(vmem_limit_bytes=size << 20)


def far(*dims):
    return pltpu.HBM(dims, f32)


def held(arrays, space):
    return [pltpu.with_memory_space_constraint(a, space) for a in arrays]


def call(kernel, outs, *args, scratch=(), close=True):
    if close:
        args = held(args, pltpu.VMEM)
    return pl.pallas_call(kernel, out_shape=outs, scratch_shapes=list(scratch), compiler_params=room(8))(*args)


def exchange_all(value):
    tiles = value.shape[0] // PEERS
    blocks = value.reshape(PEERS, 1, tiles * PEERS)
    blocks = lax.all_to_all(blocks, both, split_axis=0, concat_axis=0, tiled=True)
    return blocks.reshape(tiles * PEERS, PEERS)


def exchange_row(value):
    return lax.all_to_all(value, "gx", split_axis=0, concat_axis=0, tiled=True)


def shifted(value, axis, steps):
    count = lax.axis_size(axis)
    return lax.ppermute(value, axis, [(source, (source + steps) % count) for source in range(count)])


def pack(zone_table, velocity, stress, zones):
    whole = pl.BlockSpec(memory_space=pltpu.HBM)
    field = pltpu.VMEM((2, 3, 64, PEERS), f32)
    return pl.pallas_call(
        pack_kernel,
        in_specs=[pl.BlockSpec(memory_space=pltpu.SMEM), whole, whole, whole],
        out_shape=near(GX, PEERS, PEERS),
        scratch_shapes=[field] * 4 + [pltpu.VMEM((2, 64, PEERS), jnp.int32), pltpu.SemaphoreType.DMA((2, 5))],
        compiler_params=room(16),
        name="pack",
    )(*held((zone_table, velocity, stress, zones), pltpu.HBM))


def zones_of(zone_table, zones, stress):
    whole = lambda *dims: pl.BlockSpec(dims, lambda i: (0,) * len(dims))
    return pl.pallas_call(
        zones_kernel,
        grid=(1,),
        in_specs=[
            pl.BlockSpec(memory_space=pltpu.SMEM),
            whole(4, 64, PEERS),
            pl.BlockSpec((3, 1, 4, 64, PEERS), lambda i: (0, 0, 0, 0, 0)),
            pl.BlockSpec((3, 1, 4, 8, PEERS), lambda i: (0, 1, 0, 7, 0)),
        ],
        out_specs=[whole(3, 4, 64, PEERS), whole(64, PEERS), whole(16, PEERS)],
        out_shape=[far(3, 4, 64, PEERS), far(64, PEERS), far(16, PEERS)],
        compiler_params=room(16),
        name="zones",
    )(*held((zone_table, zones, stress, stress), pltpu.HBM))


def tails_of(history, memory, plane):
    whole = pl.BlockSpec(memory_space=pltpu.HBM)
    return pl.pallas_call(
        functools.partial(history_kernel, plane),
        in_specs=[whole, whole],
        out_shape=[far(6, 8, 1024)] * 2,
        scratch_shapes=[
            pltpu.VMEM((3, 31, 2, 8, 1024), f32),
            pltpu.VMEM((31, 8, 1024), f32),
            pltpu.SemaphoreType.DMA((10,)),
        ],
        out_specs=[pl.BlockSpec((6, 8, 1024), lambda: (0, 0, 0))] * 2,
        compiler_params=room(16),
    )(*held((history, memory), pltpu.HBM))


def steps(velocity, stress, face_mask, zones, zone_table, impedance, memory, history):
    mx, my, twist, ahead = tables()
    impedance = impedance.reshape(6, 8, 1024)
    sending, returning = near(TILES * PEERS, PEERS), near(TILES * PEERS, PEERS)
    dma = pltpu.SemaphoreType.DMA
    square = pltpu.VMEM((PEERS, PEERS), f32)

    def make_dip(carry, sent, *operands):
        spec = lambda space, count: [pl.BlockSpec(memory_space=space)] * count
        pairs = pltpu.VMEM((6, 2, 8, 1024), f32)
        outs = [returning] + [near(12, 8, 1024)] * carry
        return pl.pallas_call(
            functools.partial(dip_kernel, carry),
            in_specs=spec(pltpu.VMEM, 4) + spec(pltpu.HBM, len(operands)),
            out_specs=spec(pltpu.VMEM, len(outs)),
            out_shape=outs,
            scratch_shapes=[square] * 4 + [pltpu.VMEM((6, 8, 1024), f32), pairs, dma((6, 2))],
            compiler_params=room(8),
        )(*held((sent, my, twist, ahead), pltpu.VMEM), *held(operands, pltpu.HBM))

    def make_carry(spectrum, memory, later):
        whole = lambda *dims: pl.BlockSpec(dims, lambda i: (0,) * len(dims))
        wave = whole(6, 8, 1024)
        return pl.pallas_call(
            carry_kernel,
            grid=(1,),
            in_specs=[whole(12, 8, 1024), whole(2, 1, 8, 1024), wave, wave],
            out_specs=[wave, wave],
            out_shape=[far(6, 8, 1024)] * 2,
            compiler_params=room(8),
            name="carry",
        )(spectrum, *held((memory, *later), pltpu.HBM))

    def make_early(velocity, stress, west, south, name):
        outs = [(far if name == "early0" else near)(3, 4, 64, PEERS), far(64, PEERS), far(16, PEERS)]
        velocity, stress, coef_far = held((velocity, stress, coef), pltpu.HBM if name == "early0" else pltpu.VMEM)
        return call(early_kernel, outs, velocity, stress, west, south, coef_far, close=False)

    def make_cells(rims, early, east, north, traction, *fields):
        outs = [shape(3, 4, 64, PEERS), shape(3, 3, 4, 64, PEERS)]
        if rims:
            outs = [near(3, 4, 64, PEERS), near(3, 3, 4, 64, PEERS), far(64, PEERS), far(16, PEERS)]
            early, *fields = held((early, *fields), pltpu.HBM)
        operands = (early, east, north, traction, *fields)
        return call(functools.partial(cells_kernel, rims), outs, *operands, close=not rims)

    rows = exchange_row(pack(zone_table, velocity, stress, zones))
    coef, west, south = zones_of(zone_table, zones, stress)
    west, south = shifted(west, "gx", 1), shifted(south, "gy", 1)
    now, later = zip(tails_of(history, memory, 0), tails_of(history, memory, 1))
    sent = exchange_all(call(forward_kernel, sending, rows, mx, twist, scratch=WORK))
    onward = [((GX - 1) * GY + h, (h + 1) % GY) for h in range(GY)]
    above = lax.ppermute(rows[:, 120:], both, onward)
    early, east, north = make_early(velocity, stress, west, south, "early0")
    east, north = shifted(east, "gx", -1), shifted(north, "gy", -1)
    lines, spectrum = make_dip(True, sent, impedance, *now)
    later = make_carry(spectrum, memory, later)
    lines = exchange_all(lines)
    feed = call(feed_kernel, near(GX, 64, PEERS), rows, above)
    sending1, traction = call(
        turn_kernel,
        [sending, near(GX, 64, PEERS)],
        lines, feed, mx, twist,
        scratch=[square] * 2 + [pltpu.VMEM((GX, 48, PEERS), f32)],
    )
    sent = exchange_all(sending1)
    traction = exchange_row(traction)
    (lines,) = make_dip(False, sent, impedance, *later)
    lines = exchange_all(lines)
    velocity, stress, west, south = make_cells(True, early, east, north, traction, coef, stress, face_mask)
    west, south = shifted(west, "gx", 1), shifted(south, "gy", 1)
    early, east, north = make_early(velocity, stress, west, south, "early1")
    east, north = shifted(east, "gx", -1), shifted(north, "gy", -1)
    traction = call(inverse_kernel, near(GX, 64, PEERS), lines, mx, twist, scratch=[square] * 2)
    traction = exchange_row(traction)
    velocity, stress = make_cells(False, early, east, north, traction, coef, stress, face_mask)
    return (velocity, stress)


def solution(mesh):
    in_specs = (
        P(None, None, "gy", "gx"),
        P(None, None, None, "gy", "gx"),
        P(None, None, "gy", "gx"),
        P(None, "gy", "gx"),
        P(),
        P(None, None, both, None),
        P(None, None, both, None),
        P(None, None, None, None, both, None),
    )
    out_specs = (P(None, None, "gy", "gx"), P(None, None, None, "gy", "gx"))
    return jax.shard_map(steps, mesh=mesh, in_specs=in_specs, out_specs=out_specs, check_vma=False)
```
